32 devices in a mesh: dp: 4 (over y, core), mp: 8 (over z, x).
Axes of the slice: x: 2, y: 2, z: 4, core: 2. Of those that a mesh axis runs over, the one named last changes fastest.
Arguments:
- tokens: bfloat16 [768, 8192], P('dp', 'mp'), may hold values from -6 to 6
- out_grad: bfloat16 [768, 8192], P('dp', 'mp'), may hold values from -6 to 6
- w_gate: bfloat16 [8, 96, 128, 128], P('mp'), may hold values from -0.125 to 0.125
- w_up: bfloat16 [8, 96, 128, 128], P('mp'), may hold values from -0.125 to 0.125
- w_down: bfloat16 [8, 96, 128, 128], P('mp'), may hold values from -0.125 to 0.125
- gu_rows: int32 [8, 96], P('mp'), may hold values from 0 to 63, as said below
- gu_cols: int32 [8, 96], P('mp'), may hold values from 0 to 6
- gu_count: int32 [8], P('mp'), may hold values from 24 to 96, as said below
- dn_rows: int32 [8, 96], P('mp'), may hold values from 0 to 6, as said below
- dn_cols: int32 [8, 96], P('mp'), may hold values from 0 to 63
- dn_count: int32 [8], P('mp'), may hold values from 24 to 96, as said below
Outputs:
- ffn_out: bfloat16 [768, 8192], P('dp', 'mp')
- input_grad: bfloat16 [768, 8192], P('dp', 'mp')
- gate_step: float32 [8, 96, 128, 128], P('mp', 'dp')
- up_step: float32 [8, 96, 128, 128], P('mp', 'dp')
- down_step: float32 [8, 96, 128, 128], P('mp', 'dp')
The draws below stay inside these ranges and needn't reach their ends.
Inputs may be any that keep to these rules, and one draw needn't show every extreme that they name: Pairs (gu_rows, gu_cols) are distinct within one mp index, slots that are not live included. `gu_count`: some mp index has all 96 slots live. Pairs (dn_rows, dn_cols) are distinct within one mp index, slots that are not live included. `dn_count`: some mp index has all 96 slots live.
All inputs are finite; a program needn't handle non-finite values.
Results may differ from the reference program's by a relative error of at most 0.012.
Values may be sent and summed in bfloat16 or wider, within the bound.
A program may use at most 128 MiB of HBM per device.

```python
import math
import jax
import jax.numpy as jnp
from jax import lax

D = 8192
BLK = 128
HID_DEV = 896
MAXB = 96
TOK_DEV = 192
FF = 7168
TOKENS = 768
N_DP = 4
N_MP = 8


def live_blocks(key, salt):
    key = jax.random.fold_in(key, salt)
    key_perm, key_count, key_top = jax.random.split(key, 3)
    candidates = D // BLK * (HID_DEV // BLK)
    picks = jax.vmap(lambda k: jax.random.permutation(k, candidates))(jax.random.split(key_perm, N_MP))
    picks = picks[:, :MAXB]
    counts = jax.random.randint(key_count, (N_MP,), MAXB // 4, MAXB + 1)
    top_index = jax.random.randint(key_top, (), 0, N_MP)
    counts = jnp.where(jnp.arange(N_MP) == top_index, MAXB, counts)
    return (picks.astype(jnp.int32), counts.astype(jnp.int32))


def draw_gu_rows(key, part):
    picks, counts = live_blocks(key, 11)
    return picks // (HID_DEV // BLK)


def draw_gu_cols(key, part):
    picks, counts = live_blocks(key, 11)
    return picks % (HID_DEV // BLK)


def draw_gu_count(key, part):
    picks, counts = live_blocks(key, 11)
    return counts


def draw_dn_rows(key, part):
    picks, counts = live_blocks(key, 23)
    return picks % (HID_DEV // BLK)


def draw_dn_cols(key, part):
    picks, counts = live_blocks(key, 23)
    return picks // (HID_DEV // BLK)


def draw_dn_count(key, part):
    picks, counts = live_blocks(key, 23)
    return counts


def level_of(key, shape, cuts, least, top_value):
    gain, own = 1.0, jax.random.fold_in(key, 6)
    for axis_at, blocks in cuts:
        steps = jnp.exp(jax.random.uniform(jax.random.fold_in(own, axis_at), (blocks,), jnp.float32, least / len(cuts), top_value / len(cuts)))
        gain = gain * jnp.repeat(steps, shape[axis_at] // blocks).reshape([-1 if axis == axis_at else 1 for axis in range(len(shape))])
    return gain


def normal_values(stream_key, shape, deviation, most, shards=(), kind=jnp.bfloat16):
    drawn = deviation * jax.random.normal(stream_key, shape, jnp.float32)
    if shards:
        drawn = drawn * level_of(stream_key, shape, shards, -0.22, 0.18)
    return jnp.clip(drawn, -most, most).astype(kind)


def setup_inputs(seed: int = 0) -> dict:
    key_of = jax.random.split(jax.random.key(seed), 12)
    return {
        "tokens": normal_values(key_of[0], (TOKENS, D), 1.0, 6.0, ((0, 4), (1, 8))),
        "out_grad": normal_values(key_of[1], (TOKENS, D), 1.0, 6.0, ((0, 4), (1, 8))),
        "w_gate": normal_values(key_of[2], (N_MP, MAXB, BLK, BLK), (D // 4) ** -0.5, 0.125, ((0, 8),)),
        "w_up": normal_values(key_of[3], (N_MP, MAXB, BLK, BLK), (D // 4) ** -0.5, 0.125, ((0, 8),)),
        "w_down": normal_values(key_of[4], (N_MP, MAXB, BLK, BLK), (FF // 4) ** -0.5, 0.125, ((0, 8),)),
        "gu_rows": draw_gu_rows(jax.random.fold_in(key_of[11], 71), 0),
        "gu_cols": draw_gu_cols(jax.random.fold_in(key_of[11], 71), 0),
        "gu_count": draw_gu_count(jax.random.fold_in(key_of[11], 71), 0),
        "dn_rows": draw_dn_rows(jax.random.fold_in(key_of[11], 71), 0),
        "dn_cols": draw_dn_cols(jax.random.fold_in(key_of[11], 71), 0),
        "dn_count": draw_dn_count(jax.random.fold_in(key_of[11], 71), 0),
    }


decay_coef = 8.0

def place(count_rows, blocks, index, tiles):
    return jnp.zeros((tiles.shape[0], count_rows, blocks), jnp.float32).at[:, index, :].add(tiles)

def reference(tokens, out_grad, w_gate, w_up, w_down, gu_rows, gu_cols, gu_count, dn_rows, dn_cols, dn_count):
    hi = lax.Precision.HIGHEST
    dblocks = D // BLK
    hblocks = HID_DEV // BLK
    ntok = tokens.shape[0]
    x_blocks = tokens.astype(jnp.float32).reshape(ntok, dblocks, BLK)
    dy_blocks = out_grad.astype(jnp.float32).reshape(ntok, dblocks, BLK)
    scale_root = 1.0 / math.sqrt(TOKENS)
    slot_ids = jnp.arange(MAXB)

    def group_grad(left, right):
        left_g = left.reshape(N_DP, TOK_DEV, MAXB, BLK)
        right_g = right.reshape(N_DP, TOK_DEV, MAXB, BLK)
        parts = jnp.einsum('dtsk,dtsn->dskn', left_g, right_g, precision=hi).astype(jnp.bfloat16)
        parts = lax.optimization_barrier(parts)
        return lax.optimization_barrier(jnp.sum(parts.astype(jnp.float32), axis=0))

    def one_device(carry, m):
        out_total, in_total = carry
        wg = w_gate[m].astype(jnp.float32)
        wu = w_up[m].astype(jnp.float32)
        wd = w_down[m].astype(jnp.float32)
        rows = gu_rows[m]
        cols = gu_cols[m]
        drows = dn_rows[m]
        dcols = dn_cols[m]
        live = (slot_ids < gu_count[m]).astype(jnp.float32)
        dlive = (slot_ids < dn_count[m]).astype(jnp.float32)
        xt = x_blocks[:, rows, :]
        gate = place(hblocks, BLK, cols, jnp.einsum('tsk,skn->tsn', xt, wg, precision=hi) * live[None, :, None])
        up = place(hblocks, BLK, cols, jnp.einsum('tsk,skn->tsn', xt, wu, precision=hi) * live[None, :, None])
        sig = jax.nn.sigmoid(gate)
        act = gate * sig
        hidden = (act * up).astype(jnp.bfloat16).astype(jnp.float32)
        ht = hidden[:, drows, :]
        out_part = place(dblocks, BLK, dcols, jnp.einsum('tsk,skn->tsn', ht, wd, precision=hi) * dlive[None, :, None])
        dyt = dy_blocks[:, dcols, :]
        dhid = place(hblocks, BLK, drows, jnp.einsum('tsn,skn->tsk', dyt, wd, precision=hi) * dlive[None, :, None])
        d_gate = (dhid * up * sig * (1.0 + gate * (1.0 - sig))).astype(jnp.bfloat16).astype(jnp.float32)
        d_up = (dhid * act).astype(jnp.bfloat16).astype(jnp.float32)
        dgt = d_gate[:, cols, :]
        dut = d_up[:, cols, :]
        back = jnp.einsum('tsn,skn->tsk', dgt, wg, precision=hi) + jnp.einsum('tsn,skn->tsk', dut, wu, precision=hi)
        in_part = place(dblocks, BLK, rows, back * live[None, :, None])
        gate_grad = group_grad(xt, dgt)
        up_grad = group_grad(xt, dut)
        down_grad = group_grad(ht, dyt)
        gate_step = (gate_grad * scale_root + decay_coef * wg) * live[:, None, None]
        up_step = (up_grad * scale_root + decay_coef * wu) * live[:, None, None]
        down_step = (down_grad * scale_root + decay_coef * wd) * dlive[:, None, None]
        return ((out_total + out_part, in_total + in_part), (gate_step, up_step, down_step))
    start = (jnp.zeros((ntok, dblocks, BLK), jnp.float32), jnp.zeros((ntok, dblocks, BLK), jnp.float32))
    sums, steps = lax.scan(one_device, start, jnp.arange(N_MP).astype(jnp.int32))
    ffn_out = sums[0].reshape(ntok, D).astype(jnp.bfloat16)
    input_grad = sums[1].reshape(ntok, D).astype(jnp.bfloat16)
    return (ffn_out, input_grad, steps[0], steps[1], steps[2])
```

```python
import functools
import math

import jax
import jax.numpy as jnp
from jax import lax
from jax.experimental import pallas as pl
from jax.experimental.pallas import tpu as pltpu
from jax.sharding import PartitionSpec as P

HID_DEV = 896
MESH = pl.DeviceIdType.MESH
F32 = jnp.float32
BF16 = jnp.bfloat16

decay_coef = 8.0


def dot(left, right, contract):
    return lax.dot_general(left, right, (contract, ((), ())), preferred_element_type=F32)


def loop(lo, hi, fn):
    def body(i, carry):
        fn(i)
        return carry

    lax.fori_loop(lo, hi, body, 0)


def cross_first(per):
    return max(1, per // 4)


def slot_parts(share):
    return 3 if share % 3 == 0 else 1


def layer_kernel(
    n, nd, gtab_ref, dtab_ref, rows_ref, cols_ref, drows_ref, dcols_ref,
    x_ref, dy_ref, wg_ref, wu_ref, wd_ref,
    out_ref, in_ref, sum_ref,
    xs, dys, wgs, wus, wds, gu_acc, dh_acc, hid, dgu, hid_tiles, dgu_tiles,
    part_o, part_i, line_o, line_i, both_o, both_i, side_o, side_i, last_o, last_i,
    grad, pair, far,
    own_sem, w_sem,
    gx_send, gx_recv, gxx_send, gxx_recv, gl_send, gl_recv, glx_send, glx_recv,
    rx_send, rx_recv, rxx_send, rxx_recv, rl_send, rl_recv, rlx_send, rlx_recv,
    pair_send, pair_recv, far_send, far_recv,
):
    blk = wg_ref.shape[-1]
    ntok, width = x_ref.shape
    per = width // blk
    hblocks = gu_acc.shape[0]
    nz = n // 2
    xb = cross_first(per)
    zb = per - xb
    me = lax.axis_index("mp")
    z, x = me // 2, me % 2
    other = 1 - x
    across = {"mp": 2 * z + other}
    up = {"mp": 2 * ((z + 1) % nz) + x}
    down = {"mp": 2 * ((z + nz - 1) % nz) + x}
    toward = (up, down)
    has = (z < nz - 1, z > 0)
    dp = lax.axis_index("dp")
    ny = nd // 2
    y, core = dp // 2, dp % 2
    partner = 2 * y + (1 - core)
    ahead = 2 * ((y + 1) % ny) + core
    behind = 2 * ((y + ny - 1) % ny) + core

    barrier = pltpu.get_barrier_semaphore()
    greet = [across, up, down, {"dp": partner}, {"dp": ahead}]
    if ny > 2:
        greet.append({"dp": behind})
    for device in greet:
        pl.semaphore_signal(barrier, inc=1, device_id=device, device_id_type=MESH)

    full = (xs, dys)
    owns = [
        pltpu.make_async_copy(
            shard.at[:, pl.ds(f * blk, blk)], full[a].at[me * per + f], own_sem.at[a, f]
        )
        for a, shard in enumerate((x_ref, dy_ref))
        for f in range(per)
    ]
    loads = [
        pltpu.make_async_copy(w, held.at[pl.ds(1, w.shape[0])], w_sem.at[k])
        for k, (w, held) in enumerate(((wg_ref, wgs), (wu_ref, wus), (wd_ref, wds)))
    ]
    for copy in owns + loads:
        copy.start()

    def remote(src, dst, send, recv, device):
        return pltpu.make_async_remote_copy(
            src_ref=src, dst_ref=dst, send_sem=send, recv_sem=recv,
            device_id=device, device_id_type=MESH,
        )

    def zstart(o, c):
        return (2 * o + c) * per + c * xb

    def bstart(o):
        return (2 * o + 1) * per - xb

    def xstart(o, c):
        return (2 * o + 1) * per - (1 - c) * xb

    def gx(a, o):
        r = full[a].at[pl.ds(zstart(o, x), zb)]
        return remote(r, r, gx_send.at[a, o], gx_recv.at[a, o], across)

    def gxx(a):
        r = full[a].at[pl.ds(xstart(z, x), xb)]
        return remote(r, r, gxx_send.at[a], gxx_recv.at[a], across)

    def gl(a, o, j):
        r = full[a].at[pl.ds(zstart(o, x), zb)]
        return remote(r, r, gl_send.at[a, j, o], gl_recv.at[a, o], toward[j])

    def glx(a, o, j):
        r = full[a].at[pl.ds(bstart(o), 2 * xb)]
        return remote(r, r, glx_send.at[a, j, o], glx_recv.at[a, o], toward[j])

    def gather_begin(a):
        for j in range(2):
            @pl.when(has[j])
            def _():
                gl(a, z, j).start()
        gx(a, z).start()
        gxx(a).start()

    def gather_step(a, s):
        for j in range(2):
            o = z - s if j == 0 else z + s

            @pl.when((s > 0) & (o >= 0) & (o < nz))
            def _():
                gl(a, o, j).wait_recv()

                @pl.when(has[j])
                def _():
                    gl(a, o, j).start()

                gx(a, o).start()

        @pl.when(s == 1)
        def _():
            gxx(a).wait_recv()
            for j in range(2):
                @pl.when(has[j])
                def _():
                    glx(a, z, j).start()

        for j in range(2):
            o = z - (s - 1) if j == 0 else z + (s - 1)

            @pl.when((s > 1) & (o >= 0) & (o < nz))
            def _():
                glx(a, o, j).wait_recv()

                @pl.when(has[j])
                def _():
                    glx(a, o, j).start()

    def gather_work(a, s, work):
        def side(j):
            sign = 2 * j - 1
            near = z + sign * s
            late = z + sign * (s - 1)

            @pl.when((near >= 0) & (near < nz) & ((s > 0) | (j == 0)))
            def _():
                work(zstart(near, x), zb)

            @pl.when((s > 0) & (late >= 0) & (late < nz) & ((s > 1) | (j == 0)))
            def _():
                gx(a, late).wait_recv()
                work(zstart(late, other), zb)
                work(bstart(late), 2 * xb)

        loop(0, 2, side)

    def gather_done(a):
        def body(o):
            gx(a, o).wait_send()
            for j in range(2):
                passed = (o <= z) if j == 0 else (o >= z)

                @pl.when(has[j] & passed)
                def _():
                    gl(a, o, j).wait_send()
                    glx(a, o, j).wait_send()

        loop(0, nz, body)
        gxx(a).wait_send()

    def features(a, start, count):
        return jnp.concatenate([full[a][start + f] for f in range(count)], axis=1)

    def gate_up(start, count):
        left = features(0, start, count)
        for h in range(hblocks):
            tabs = [gtab_ref[(start + f) * hblocks + h] for f in range(count)]
            rhs = jnp.concatenate(
                [jnp.concatenate([wgs[t], wus[t]], axis=1) for t in tabs], axis=0
            )
            gu_acc[h] += dot(left, rhs, ((1,), (0,)))

    def hidden_back(start, count):
        left = features(1, start, count)
        for h in range(0, hblocks, 2):
            hs = range(h, min(h + 2, hblocks))
            rhs = jnp.concatenate(
                [
                    jnp.concatenate(
                        [wds[dtab_ref[(start + f) * hblocks + k]] for f in range(count)], axis=1
                    )
                    for k in hs
                ],
                axis=0,
            )
            got = dot(left, rhs, ((1,), (1,)))
            for i, k in enumerate(hs):
                dh_acc[k] += got[:, i * blk:(i + 1) * blk]

    part = (part_o, part_i)
    line = (line_o, line_i)
    both = (both_o, both_i)
    side_in = (side_o, side_i)
    last = (last_o, last_i)
    results = (out_ref, in_ref)

    def out_range(start, count):
        for i in range(0, count, 2):
            fs = range(i, min(i + 2, count))
            rhs = jnp.concatenate(
                [
                    jnp.concatenate([wds[dtab_ref[(start + f) * hblocks + h]] for f in fs], axis=1)
                    for h in range(hblocks)
                ],
                axis=0,
            )
            got = dot(hid[...], rhs, ((1,), (0,))).astype(BF16)
            for k, f in enumerate(fs):
                part_o[start + f] = got[:, k * blk:(k + 1) * blk]

    def in_range(start, count):
        for i in range(0, count, 2):
            fs = range(i, min(i + 2, count))
            rhs = jnp.concatenate(
                [
                    jnp.concatenate(
                        [
                            held[t]
                            for t in [gtab_ref[(start + f) * hblocks + h] for h in range(hblocks)]
                            for held in (wgs, wus)
                        ],
                        axis=1,
                    )
                    for f in fs
                ],
                axis=0,
            )
            got = dot(dgu[...], rhs, ((1,), (1,))).astype(BF16)
            for k, f in enumerate(fs):
                part_i[start + f] = got[:, k * blk:(k + 1) * blk]

    ranges = (out_range, in_range)

    def rx(a, o):
        return remote(
            part[a].at[pl.ds(zstart(o, other), zb)], side_in[a].at[o],
            rx_send.at[a, o], rx_recv.at[a, o], across,
        )

    def rxx(a):
        return remote(
            part[a].at[pl.ds(xstart(z, other), xb)], last[a],
            rxx_send.at[a], rxx_recv.at[a], across,
        )

    def place(o, j):
        if j == 0:
            return o
        return jnp.where(o == z - 1, nz, o)

    def rl(a, o, j):
        slot = place(o, j)
        return remote(
            part[a].at[pl.ds(zstart(o, x), zb)], line[a].at[slot],
            rl_send.at[a, o], rl_recv.at[a, slot], toward[j],
        )

    def rlx(a, o, j):
        slot = place(o, j)
        return remote(
            part[a].at[pl.ds(bstart(o), 2 * xb)], both[a].at[slot],
            rlx_send.at[a, o], rlx_recv.at[a, slot], toward[j],
        )

    def line_wait(a, slot):
        remote(
            part[a].at[pl.ds(0, zb)], line[a].at[slot], rl_send.at[a, 0], rl_recv.at[a, slot], up
        ).wait_recv()

    def both_wait(a, slot):
        remote(
            part[a].at[pl.ds(0, 2 * xb)], both[a].at[slot], rlx_send.at[a, 0], rlx_recv.at[a, slot], up
        ).wait_recv()

    def dest(t, j):
        o = nz - t + z if j == 0 else t + z - nz
        return o, (o >= 0) & (o < nz) & (t < nz)

    def both_add(a, o, slot):
        base = bstart(o)

        def body(i):
            part[a][base + i] = (part[a][base + i].astype(F32) + both[a][slot, i].astype(F32)).astype(BF16)

        loop(0, 2 * xb, body)

    def both_work(a):
        loop(0, nz, lambda o: ranges[a](bstart(o), 2 * xb))

    def both_step(a, t):
        for j in range(2):
            o, valid = dest(t, j)

            @pl.when(valid)
            def _():
                @pl.when(has[1 - j])
                def _():
                    both_wait(a, o)
                    both_add(a, o, o)

                rlx(a, o, j).start()

    def both_final(a):
        @pl.when(z > 0)
        def _():
            both_wait(a, z)
            both_add(a, z, z)

        @pl.when(z < nz - 1)
        def _():
            both_wait(a, nz)
            both_add(a, z, nz)

        rxx(a).start()

    def line_work(a, t):
        def body(j):
            o = jnp.where(j == 0, nz - t + z, t + z - nz)

            @pl.when((o >= 0) & (o < nz) & ((j == 0) | (t < nz)))
            def _():
                ranges[a](zstart(o, other), zb)
                rx(a, o).start()
                ranges[a](zstart(o, x), zb)

        loop(0, 2, body)

    def line_step(a, t):
        for j in range(2):
            o, valid = dest(t, j)

            @pl.when(valid)
            def _():
                rx(a, o).wait_recv()
                base = zstart(o, x)

                @pl.when(has[1 - j])
                def _():
                    line_wait(a, o)

                    def body(i):
                        part[a][base + i] = (
                            part[a][base + i].astype(F32)
                            + side_in[a][o, i].astype(F32)
                            + line[a][o, i].astype(F32)
                        ).astype(BF16)

                    loop(0, zb, body)

                @pl.when(jnp.logical_not(has[1 - j]))
                def _():
                    def body(i):
                        part[a][base + i] = (
                            part[a][base + i].astype(F32) + side_in[a][o, i].astype(F32)
                        ).astype(BF16)

                    loop(0, zb, body)

                rl(a, o, j).start()

    def line_final(a):
        rx(a, z).wait_recv()
        base = zstart(z, x)

        def lanes(i):
            return pl.ds(pl.multiple_of((x * xb + i) * blk, blk), blk)

        def finish_line(slots):
            for slot in slots:
                line_wait(a, slot)

            def body(i):
                total = part[a][base + i].astype(F32) + side_in[a][z, i].astype(F32)
                for slot in slots:
                    total = total + line[a][slot, i].astype(F32)
                results[a][:, lanes(i)] = total.astype(BF16)

            loop(0, zb, body)

        @pl.when(z == 0)
        def _():
            finish_line([nz])

        @pl.when(z == nz - 1)
        def _():
            finish_line([z])

        @pl.when((z > 0) & (z < nz - 1))
        def _():
            finish_line([z, nz])

        rxx(a).wait_recv()

        def body(i):
            at = pl.ds(pl.multiple_of((other * zb + i) * blk, blk), blk)
            total = part[a][xstart(z, x) + i].astype(F32) + last[a][i].astype(F32)
            results[a][:, at] = total.astype(BF16)

        loop(0, xb, body)

    def scatter_done(a):
        def body(o):
            rx(a, o).wait_send()
            for j in range(2):
                passed = (o > z) if j == 0 else (o < z)

                @pl.when(passed)
                def _():
                    rl(a, o, j).wait_send()
                    rlx(a, o, j).wait_send()

        loop(0, nz, body)
        rxx(a).wait_send()

    parts, bunch = grad.shape[2], grad.shape[4]

    def group(t):
        return (y + 2 * ny - 1 - t) % ny

    def slot_grads(t, c, q):
        g = group(t)
        base = (2 * g + c) * parts * bunch + q * bunch
        unit = 4

        def body(i):
            for j in range(unit):
                e = i * unit + j
                s = base + e
                down_grad = dot(hid_tiles[drows_ref[s]], dys[dcols_ref[s]], ((0,), (0,)))
                pair_grad = dot(xs[rows_ref[s]], dgu_tiles[cols_ref[s]], ((0,), (0,)))
                grad[g, c, q, 0, e] = pair_grad[:, :blk].astype(BF16)
                grad[g, c, q, 1, e] = pair_grad[:, blk:].astype(BF16)
                grad[g, c, q, 2, e] = down_grad.astype(BF16)

        loop(0, bunch // unit, body)

    pairs = {}
    fars = {}

    def give(t, q):
        slot_grads(t, 1 - core, q)
        g = group(t)
        pairs[t, q] = remote(
            grad.at[g, 1 - core, q], pair.at[g, q],
            pair_send.at[t, q], pair_recv.at[t, q], {"dp": partner},
        )
        pairs[t, q].start()

    def keep(t, q):
        slot_grads(t, core, q)

    def pair_add(t, q):
        g = group(t)
        pairs[t, q].wait_recv()
        if t > 0:
            fars[t - 1, q].wait_recv()
        for k in range(3):
            def body(i):
                total = pair[g, q, k, i].astype(F32) + grad[g, core, q, k, i].astype(F32)
                if t > 0:
                    total = total + far[t - 1, q, k, i].astype(F32)
                if t < ny - 1:
                    pair[g, q, k, i] = total.astype(BF16)
                else:
                    sum_ref[k, q * bunch + i] = total

            loop(0, bunch, body)
        if t < ny - 1:
            fars[t, q] = remote(
                pair.at[g, q], far.at[t, q], far_send.at[t, q], far_recv.at[t, q], {"dp": ahead}
            )
            fars[t, q].start()

    gu_acc[...] = jnp.zeros_like(gu_acc)
    dh_acc[...] = jnp.zeros_like(dh_acc)
    for held in (wgs, wus, wds):
        held[0] = jnp.zeros((blk, blk), BF16)
    for copy in owns[:per]:
        copy.wait()
    pl.semaphore_wait(barrier, len(greet))
    gather_begin(0)
    for copy in loads + owns[per:]:
        copy.wait()

    def tokens_step(s):
        gather_step(0, s)

        @pl.when(s == nz - 1)
        def _():
            gather_begin(1)

        gather_work(0, s, gate_up)

    loop(0, nz + 1, tokens_step)

    for h in range(hblocks):
        gate = gu_acc[h, :, :blk]
        sig = 1.0 / (1.0 + jnp.exp(-gate))
        hidden = (gate * sig * gu_acc[h, :, blk:]).astype(BF16)
        hid[:, h * blk:(h + 1) * blk] = hidden
        hid_tiles[h] = hidden

    both_work(0)

    def cotangent_step(s):
        gather_step(1, s)

        @pl.when(s > 0)
        def _():
            both_step(0, s)
            line_work(0, s)

        gather_work(1, s, hidden_back)

        @pl.when(s > 1)
        def _():
            line_step(0, s - 1)

    loop(0, nz + 1, cotangent_step)

    for h in range(hblocks):
        gate = gu_acc[h, :, :blk]
        up_part = gu_acc[h, :, blk:]
        dhid = dh_acc[h]
        sig = 1.0 / (1.0 + jnp.exp(-gate))
        act = gate * sig
        d_gate = (dhid * up_part * sig * (1.0 + gate * (1.0 - sig))).astype(BF16)
        d_up = (dhid * act).astype(BF16)
        two = jnp.concatenate([d_gate, d_up], axis=1)
        dgu[:, 2 * h * blk:2 * (h + 1) * blk] = two
        dgu_tiles[h] = two

    give(0, 0)
    both_work(1)
    both_step(1, 1)
    keep(0, 0)
    both_final(0)
    pair_add(0, 0)
    tasks = []
    for q in range(1, parts):
        tasks += [functools.partial(give, 0, q), functools.partial(keep, 0, q), functools.partial(pair_add, 0, q)]
    for t in range(1, ny):
        for q in range(parts):
            tasks += [functools.partial(give, t, q), functools.partial(keep, t, q)]
            if t < ny - 1:
                tasks.append(functools.partial(pair_add, t, q))

    def run(count):
        for _ in range(min(count, len(tasks))):
            tasks.pop(0)()

    quarter = nz // 4 if nz >= 4 else 1
    marks = list(range(1, nz, quarter)) + [nz]

    def scatter_steps(lo, hi):
        def body(t):
            line_work(1, t)

            @pl.when(t > 1)
            def _():
                both_step(1, t)
                line_step(1, t - 1)

        loop(lo, hi, body)

    for i, lo in enumerate(marks):
        hi = marks[i + 1] if i + 1 < len(marks) else nz + 1
        scatter_steps(lo, hi)
        if i == 0:
            line_final(0)
        if i == len(marks) - 1:
            both_final(1)
        run(3)
    for task in tasks:
        task()
    line_final(1)
    for q in range(parts):
        pair_add(ny - 1, q)
    for a in range(2):
        gather_done(a)
        scatter_done(a)
    for copy in list(pairs.values()) + list(fars.values()):
        copy.wait_send()


def layer(tokens, out_grad, wg, wu, wd, gtab, dtab, rows, cols, drows, dcols, n, nd):
    ntok, width = tokens.shape
    slots, blk, _ = wg.shape
    share = slots // nd
    ny = nd // 2
    nz = n // 2
    hblocks = HID_DEV // blk
    per = width // blk
    xb = cross_first(per)
    zb = per - xb
    parts = slot_parts(share)
    bunch = share // parts
    dma = pltpu.SemaphoreType.DMA
    return pl.pallas_call(
        functools.partial(layer_kernel, n, nd),
        out_shape=(
            jax.ShapeDtypeStruct((ntok, width), BF16),
            jax.ShapeDtypeStruct((ntok, width), BF16),
            jax.ShapeDtypeStruct((3, share, blk, blk), F32),
        ),
        in_specs=[pl.BlockSpec(memory_space=pltpu.SMEM)] * 6
        + [pl.BlockSpec(memory_space=pl.ANY)] * 5,
        out_specs=(pl.BlockSpec(memory_space=pltpu.VMEM),) * 3,
        scratch_shapes=[
            pltpu.VMEM((n * per, ntok, blk), BF16),
            pltpu.VMEM((n * per, ntok, blk), BF16),
            pltpu.VMEM((slots + 1, blk, blk), BF16),
            pltpu.VMEM((slots + 1, blk, blk), BF16),
            pltpu.VMEM((slots + 1, blk, blk), BF16),
            pltpu.VMEM((hblocks, ntok, 2 * blk), F32),
            pltpu.VMEM((hblocks, ntok, blk), F32),
            pltpu.VMEM((ntok, hblocks * blk), BF16),
            pltpu.VMEM((ntok, 2 * hblocks * blk), BF16),
            pltpu.VMEM((hblocks, ntok, blk), BF16),
            pltpu.VMEM((hblocks, ntok, 2 * blk), BF16),
            pltpu.VMEM((n * per, ntok, blk), BF16),
            pltpu.VMEM((n * per, ntok, blk), BF16),
            pltpu.VMEM((nz + 1, zb, ntok, blk), BF16),
            pltpu.VMEM((nz + 1, zb, ntok, blk), BF16),
            pltpu.VMEM((nz + 1, 2 * xb, ntok, blk), BF16),
            pltpu.VMEM((nz + 1, 2 * xb, ntok, blk), BF16),
            pltpu.VMEM((nz, zb, ntok, blk), BF16),
            pltpu.VMEM((nz, zb, ntok, blk), BF16),
            pltpu.VMEM((xb, ntok, blk), BF16),
            pltpu.VMEM((xb, ntok, blk), BF16),
            pltpu.VMEM((ny, 2, parts, 3, bunch, blk, blk), BF16),
            pltpu.VMEM((ny, parts, 3, bunch, blk, blk), BF16),
            pltpu.VMEM((max(ny - 1, 1), parts, 3, bunch, blk, blk), BF16),
            dma((2, per)),
            dma((3,)),
            dma((2, nz)), dma((2, nz)), dma((2,)), dma((2,)),
            dma((2, 2, nz)), dma((2, nz)), dma((2, 2, nz)), dma((2, nz)),
            dma((2, nz)), dma((2, nz)), dma((2,)), dma((2,)),
            dma((2, nz)), dma((2, nz + 1)), dma((2, nz)), dma((2, nz + 1)),
            dma((ny, parts)), dma((ny, parts)), dma((ny, parts)), dma((ny, parts)),
        ],
        compiler_params=pltpu.CompilerParams(
            collective_id=0, has_side_effects=True, vmem_limit_bytes=60 << 20
        ),
    )(gtab, dtab, rows, cols, drows, dcols, tokens, out_grad, wg, wu, wd)


def slot_table(features, hidden, count, dblocks, hblocks):
    slot = jnp.arange(features.shape[0])
    key = jnp.where(slot < count[0], features * hblocks + hidden, -1)
    hit = key[None, :] == jnp.arange(dblocks * hblocks)[:, None]
    return jnp.sum(jnp.where(hit, slot[None, :] + 1, 0), axis=1).astype(jnp.int32)


def finish(summed, weights, count, scale_root):
    share = summed.shape[0]
    start = lax.axis_index("dp") * share
    own_w = lax.dynamic_slice_in_dim(weights, start, share, 0).astype(F32)
    live = start + jnp.arange(share) < count[0]
    return jnp.where(live[:, None, None], summed * scale_root + decay_coef * own_w, 0.0)[None]


def local(
    tokens, out_grad, w_gate, w_up, w_down, gu_rows, gu_cols, gu_count, dn_rows, dn_cols, dn_count
):
    n = lax.axis_size("mp")
    nd = lax.axis_size("dp")
    wg, wu, wd = w_gate[0], w_up[0], w_down[0]
    scale_root = 1.0 / math.sqrt(tokens.shape[0] * nd)
    blk = wg.shape[-1]
    dblocks = tokens.shape[1] * n // blk
    hblocks = HID_DEV // blk
    gtab = slot_table(gu_rows[0], gu_cols[0], gu_count, dblocks, hblocks)
    dtab = slot_table(dn_cols[0], dn_rows[0], dn_count, dblocks, hblocks)
    ffn_out, input_grad, summed = layer(
        tokens, out_grad, wg, wu, wd, gtab, dtab,
        gu_rows[0], gu_cols[0], dn_rows[0], dn_cols[0], n, nd,
    )
    gate_step = finish(summed[0], wg, gu_count, scale_root)
    up_step = finish(summed[1], wu, gu_count, scale_root)
    down_step = finish(summed[2], wd, dn_count, scale_root)
    return (ffn_out, input_grad, gate_step, up_step, down_step)


def solution(mesh):
    in_specs = (
        P("dp", "mp"),
        P("dp", "mp"),
        P("mp", None, None, None),
        P("mp", None, None, None),
        P("mp", None, None, None),
        P("mp", None),
        P("mp", None),
        P("mp"),
        P("mp", None),
        P("mp", None),
        P("mp"),
    )
    out_specs = (
        P("dp", "mp"),
        P("dp", "mp"),
        P("mp", "dp", None, None),
        P("mp", "dp", None, None),
        P("mp", "dp", None, None),
    )
    return jax.shard_map(local, mesh=mesh, in_specs=in_specs, out_specs=out_specs, check_vma=False)
```

```python
import functools
import math

import jax
import jax.numpy as jnp
from jax import lax
from jax.experimental import pallas as pl
from jax.experimental.pallas import tpu as pltpu
from jax.sharding import PartitionSpec as P

HID_DEV = 896
MESH = pl.DeviceIdType.MESH
F32 = jnp.float32
BF16 = jnp.bfloat16

decay_coef = 8.0


def dot(left, right, contract):
    return lax.dot_general(left, right, (contract, ((), ())), preferred_element_type=F32)


def loop(lo, hi, fn):
    def body(i, carry):
        fn(i)
        return carry

    lax.fori_loop(lo, hi, body, 0)


CROSS_FIRST = {"tokens": 1, "out_grad": 1, "ffn_out": 4, "input_grad": 3}


def cross_first(per, name):
    return max(1, per * CROSS_FIRST[name] // 8)


def slot_parts(share):
    return 3 if share % 3 == 0 else 1


def layer_kernel(
    n, nd, scale_root, gtab_ref, dtab_ref, rows_ref, cols_ref, drows_ref, dcols_ref, gcount_ref, dcount_ref,
    x_ref, dy_ref, wg_ref, wu_ref, wd_ref,
    out_ref, in_ref, step_ref,
    xs, dys, wgs, wus, wds, gu_acc, dh_acc, hid, dgu, hid_tiles, dgu_tiles,
    part_o, part_i, line_o, line_i, both_o, both_i, side_o, side_i, last_o, last_i,
    grad, pair, far, stage,
    own_sem, w_sem,
    gx_send, gx_recv, gxx_send, gxx_recv, gl_send, gl_recv, glx_send, glx_recv,
    rx_send, rx_recv, rxx_send, rxx_recv, rl_send, rl_recv, rlx_send, rlx_recv,
    pair_send, pair_recv, far_send, far_recv,
):
    blk = wg_ref.shape[-1]
    ntok, width = x_ref.shape
    per = width // blk
    hblocks = gu_acc.shape[0]
    nz = n // 2
    gxb = (cross_first(per, "tokens"), cross_first(per, "out_grad"))
    rxb = (cross_first(per, "ffn_out"), cross_first(per, "input_grad"))
    me = lax.axis_index("mp")
    z, x = me // 2, me % 2
    other = 1 - x
    across = {"mp": 2 * z + other}
    up = {"mp": 2 * ((z + 1) % nz) + x}
    down = {"mp": 2 * ((z + nz - 1) % nz) + x}
    toward = (up, down)
    has = (z < nz - 1, z > 0)
    dp = lax.axis_index("dp")
    ny = nd // 2
    y, core = dp // 2, dp % 2
    partner = 2 * y + (1 - core)
    ahead = 2 * ((y + 1) % ny) + core
    behind = 2 * ((y + ny - 1) % ny) + core

    barrier = pltpu.get_barrier_semaphore()
    greet = [across, up, down, {"dp": partner}, {"dp": ahead}]
    if ny > 2:
        greet.append({"dp": behind})
    for device in greet:
        pl.semaphore_signal(barrier, inc=1, device_id=device, device_id_type=MESH)

    full = (xs, dys)
    owns = [
        pltpu.make_async_copy(shard, stage.at[a], own_sem.at[a])
        for a, shard in enumerate((x_ref, dy_ref))
    ]
    loads = [
        pltpu.make_async_copy(w, held.at[pl.ds(1, w.shape[0])], w_sem.at[k])
        for k, (w, held) in enumerate(((wg_ref, wgs), (wu_ref, wus), (wd_ref, wds)))
    ]
    for copy in owns:
        copy.start()

    def remote(src, dst, send, recv, device):
        return pltpu.make_async_remote_copy(
            src_ref=src, dst_ref=dst, send_sem=send, recv_sem=recv,
            device_id=device, device_id_type=MESH,
        )

    def zspan(o, c, xb):
        return pl.ds((2 * o + c) * per + c * xb, per - xb)

    def bspan(o, xb):
        return pl.ds((2 * o + 1) * per - xb, 2 * xb)

    def xspan(o, c, xb):
        return pl.ds((2 * o + 1) * per - (1 - c) * xb, xb)

    def gx(a, o):
        r = full[a].at[zspan(o, x, gxb[a])]
        return remote(r, r, gx_send.at[a, o], gx_recv.at[a, o], across)

    def gxx(a):
        r = full[a].at[xspan(z, x, gxb[a])]
        return remote(r, r, gxx_send.at[a], gxx_recv.at[a], across)

    def gl(a, o, j):
        r = full[a].at[zspan(o, x, gxb[a])]
        return remote(r, r, gl_send.at[a, j, o], gl_recv.at[a, o], toward[j])

    def glx(a, o, j):
        r = full[a].at[bspan(o, gxb[a])]
        return remote(r, r, glx_send.at[a, j, o], glx_recv.at[a, o], toward[j])

    def gather_begin(a):
        for j in range(2):
            @pl.when(has[j])
            def _():
                gl(a, z, j).start()
        gx(a, z).start()
        gxx(a).start()

    def gather_step(a, s):
        for j in range(2):
            o = z - s if j == 0 else z + s

            @pl.when((s > 0) & (o >= 0) & (o < nz))
            def _():
                gl(a, o, j).wait_recv()

                @pl.when(has[j])
                def _():
                    gl(a, o, j).start()

                gx(a, o).start()

        @pl.when(s == 1)
        def _():
            gxx(a).wait_recv()
            for j in range(2):
                @pl.when(has[j])
                def _():
                    glx(a, z, j).start()

        for j in range(2):
            o = z - (s - 1) if j == 0 else z + (s - 1)

            @pl.when((s > 1) & (o >= 0) & (o < nz))
            def _():
                glx(a, o, j).wait_recv()

                @pl.when(has[j])
                def _():
                    glx(a, o, j).start()

    def gather_work(a, s, work):
        def side(j):
            sign = 2 * j - 1
            near = z + sign * s
            late = z + sign * (s - 1)

            @pl.when((near >= 0) & (near < nz) & ((s > 0) | (j == 0)))
            def _():
                work(zspan(near, x, gxb[a]))

            @pl.when((s > 0) & (late >= 0) & (late < nz) & ((s > 1) | (j == 0)))
            def _():
                gx(a, late).wait_recv()
                work(zspan(late, other, gxb[a]))
                work(bspan(late, gxb[a]))

        loop(0, 2, side)

    def gather_done(a):
        def body(o):
            gx(a, o).wait_send()
            for j in range(2):
                passed = (o <= z) if j == 0 else (o >= z)

                @pl.when(has[j] & passed)
                def _():
                    gl(a, o, j).wait_send()
                    glx(a, o, j).wait_send()

        loop(0, nz, body)
        gxx(a).wait_send()

    def own_blocks(a):
        owns[a].wait()
        for f in range(per):
            full[a][me * per + f] = stage[a, :, f * blk:(f + 1) * blk]

    def features(a, start, count):
        return jnp.concatenate([full[a][start + f] for f in range(count)], axis=1)

    def gate_up(span):
        start, count = span.start, span.size
        left = features(0, start, count)
        for h in range(hblocks):
            tabs = [gtab_ref[(start + f) * hblocks + h] for f in range(count)]
            rhs = jnp.concatenate(
                [jnp.concatenate([wgs[t], wus[t]], axis=1) for t in tabs], axis=0
            )
            gu_acc[h] += dot(left, rhs, ((1,), (0,)))

    def hidden_back(span):
        start, count = span.start, span.size
        left = features(1, start, count)
        for h in range(0, hblocks, 2):
            hs = range(h, min(h + 2, hblocks))
            rhs = jnp.concatenate(
                [
                    jnp.concatenate(
                        [wds[dtab_ref[(start + f) * hblocks + k]] for f in range(count)], axis=1
                    )
                    for k in hs
                ],
                axis=0,
            )
            got = dot(left, rhs, ((1,), (1,)))
            for i, k in enumerate(hs):
                dh_acc[k] += got[:, i * blk:(i + 1) * blk]

    part = (part_o, part_i)
    line = (line_o, line_i)
    both = (both_o, both_i)
    side_in = (side_o, side_i)
    last = (last_o, last_i)
    results = (out_ref, in_ref)

    def out_range(span):
        start, count = span.start, span.size
        for i in range(0, count, 2):
            fs = range(i, min(i + 2, count))
            rhs = jnp.concatenate(
                [
                    jnp.concatenate([wds[dtab_ref[(start + f) * hblocks + h]] for f in fs], axis=1)
                    for h in range(hblocks)
                ],
                axis=0,
            )
            got = dot(hid[...], rhs, ((1,), (0,))).astype(BF16)
            for k, f in enumerate(fs):
                part_o[start + f] = got[:, k * blk:(k + 1) * blk]

    def in_range(span):
        start, count = span.start, span.size
        for i in range(0, count, 2):
            fs = range(i, min(i + 2, count))
            rhs = jnp.concatenate(
                [
                    jnp.concatenate(
                        [
                            held[t]
                            for t in [gtab_ref[(start + f) * hblocks + h] for h in range(hblocks)]
                            for held in (wgs, wus)
                        ],
                        axis=1,
                    )
                    for f in fs
                ],
                axis=0,
            )
            got = dot(dgu[...], rhs, ((1,), (1,))).astype(BF16)
            for k, f in enumerate(fs):
                part_i[start + f] = got[:, k * blk:(k + 1) * blk]

    ranges = (out_range, in_range)

    def rx(a, o):
        return remote(
            part[a].at[zspan(o, other, rxb[a])], side_in[a].at[o],
            rx_send.at[a, o], rx_recv.at[a, o], across,
        )

    def rxx(a):
        return remote(
            part[a].at[xspan(z, other, rxb[a])], last[a],
            rxx_send.at[a], rxx_recv.at[a], across,
        )

    def place(o, j):
        if j == 0:
            return o
        return jnp.where(o == z - 1, nz, o)

    def rl(a, o, j):
        slot = place(o, j)
        return remote(
            part[a].at[zspan(o, x, rxb[a])], line[a].at[slot],
            rl_send.at[a, o], rl_recv.at[a, slot], toward[j],
        )

    def rlx(a, o, j):
        slot = place(o, j)
        return remote(
            part[a].at[bspan(o, rxb[a])], both[a].at[slot],
            rlx_send.at[a, o], rlx_recv.at[a, slot], toward[j],
        )

    def line_wait(a, slot):
        remote(
            part[a].at[pl.ds(0, per - rxb[a])], line[a].at[slot], rl_send.at[a, 0], rl_recv.at[a, slot], up
        ).wait_recv()

    def both_wait(a, slot):
        remote(
            part[a].at[pl.ds(0, 2 * rxb[a])], both[a].at[slot], rlx_send.at[a, 0], rlx_recv.at[a, slot], up
        ).wait_recv()

    def dest(t, j):
        o = nz - t + z if j == 0 else t + z - nz
        return o, (o >= 0) & (o < nz) & (t < nz)

    def both_add(a, o, slot):
        base = bspan(o, rxb[a]).start

        def body(i):
            part[a][base + i] = (part[a][base + i].astype(F32) + both[a][slot, i].astype(F32)).astype(BF16)

        loop(0, 2 * rxb[a], body)

    def both_work(a):
        loop(0, nz, lambda o: ranges[a](bspan(o, rxb[a])))

    def both_step(a, t):
        for j in range(2):
            o, valid = dest(t, j)

            @pl.when(valid)
            def _():
                @pl.when(has[1 - j])
                def _():
                    both_wait(a, o)
                    both_add(a, o, o)

                rlx(a, o, j).start()

    def both_final(a):
        @pl.when(z > 0)
        def _():
            both_wait(a, z)
            both_add(a, z, z)

        @pl.when(z < nz - 1)
        def _():
            both_wait(a, nz)
            both_add(a, z, nz)

        rxx(a).start()

    def line_work(a, t, send):
        def body(j):
            o = jnp.where(j == 0, nz - t + z, t + z - nz)

            @pl.when((o >= 0) & (o < nz) & ((j == 0) | (t < nz)))
            def _():
                ranges[a](zspan(o, other, rxb[a]))
                if send:
                    rx(a, o).start()
                ranges[a](zspan(o, x, rxb[a]))

        loop(0, 2, body)

    def line_cross(a, t):
        for j in range(2):
            o, valid = dest(t, j)

            @pl.when(valid)
            def _():
                rx(a, o).start()

    def line_step(a, t):
        for j in range(2):
            o, valid = dest(t, j)

            @pl.when(valid)
            def _():
                rx(a, o).wait_recv()
                base = zspan(o, x, rxb[a]).start

                @pl.when(has[1 - j])
                def _():
                    line_wait(a, o)

                    def body(i):
                        part[a][base + i] = (
                            part[a][base + i].astype(F32)
                            + side_in[a][o, i].astype(F32)
                            + line[a][o, i].astype(F32)
                        ).astype(BF16)

                    loop(0, per - rxb[a], body)

                @pl.when(jnp.logical_not(has[1 - j]))
                def _():
                    def body(i):
                        part[a][base + i] = (
                            part[a][base + i].astype(F32) + side_in[a][o, i].astype(F32)
                        ).astype(BF16)

                    loop(0, per - rxb[a], body)

                rl(a, o, j).start()

    def line_final(a):
        rx(a, z).wait_recv()
        xb = rxb[a]
        zb = per - xb
        base = zspan(z, x, xb).start

        def lanes(i):
            return pl.ds(pl.multiple_of((x * xb + i) * blk, blk), blk)

        def finish_line(slots):
            for slot in slots:
                line_wait(a, slot)

            def body(i):
                total = part[a][base + i].astype(F32) + side_in[a][z, i].astype(F32)
                for slot in slots:
                    total = total + line[a][slot, i].astype(F32)
                results[a][:, lanes(i)] = total.astype(BF16)

            loop(0, zb, body)

        @pl.when(z == 0)
        def _():
            finish_line([nz])

        @pl.when(z == nz - 1)
        def _():
            finish_line([z])

        @pl.when((z > 0) & (z < nz - 1))
        def _():
            finish_line([z, nz])

        rxx(a).wait_recv()

        def body(i):
            at = pl.ds(pl.multiple_of((other * zb + i) * blk, blk), blk)
            total = part[a][xspan(z, x, xb).start + i].astype(F32) + last[a][i].astype(F32)
            results[a][:, at] = total.astype(BF16)

        loop(0, xb, body)

    def scatter_done(a):
        def body(o):
            rx(a, o).wait_send()
            for j in range(2):
                passed = (o > z) if j == 0 else (o < z)

                @pl.when(passed)
                def _():
                    rl(a, o, j).wait_send()
                    rlx(a, o, j).wait_send()

        loop(0, nz, body)
        rxx(a).wait_send()

    parts, bunch = grad.shape[2], grad.shape[4]

    def group(t):
        return (y + 2 * ny - 1 - t) % ny

    def slot_grads(t, c, q):
        g = group(t)
        base = (2 * g + c) * parts * bunch + q * bunch
        unit = 4

        def body(i):
            for j in range(unit):
                e = i * unit + j
                s = base + e
                down_grad = dot(hid_tiles[drows_ref[s]], dys[dcols_ref[s]], ((0,), (0,)))
                pair_grad = dot(xs[rows_ref[s]], dgu_tiles[cols_ref[s]], ((0,), (0,)))
                grad[g, c, q, 0, e] = pair_grad[:, :blk].astype(BF16)
                grad[g, c, q, 1, e] = pair_grad[:, blk:].astype(BF16)
                grad[g, c, q, 2, e] = down_grad.astype(BF16)

        loop(0, bunch // unit, body)

    pairs = {}
    fars = {}
    weights = (wgs, wus, wds)
    counts = (gcount_ref, gcount_ref, dcount_ref)

    def give(t, q):
        slot_grads(t, 1 - core, q)
        g = group(t)
        pairs[t, q] = remote(
            grad.at[g, 1 - core, q], pair.at[g, q],
            pair_send.at[t, q], pair_recv.at[t, q], {"dp": partner},
        )
        pairs[t, q].start()

    def keep(t, q):
        slot_grads(t, core, q)

    def pair_add(t, q):
        g = group(t)
        pairs[t, q].wait_recv()
        if t > 0:
            fars[t - 1, q].wait_recv()
        for k in range(3):
            def body(i):
                total = pair[g, q, k, i].astype(F32) + grad[g, core, q, k, i].astype(F32)
                if t > 0:
                    total = total + far[t - 1, q, k, i].astype(F32)
                if t < ny - 1:
                    pair[g, q, k, i] = total.astype(BF16)
                else:
                    slot = dp * parts * bunch + q * bunch + i
                    decayed = total * scale_root + decay_coef * weights[k][slot + 1].astype(F32)
                    step_ref[k, q * bunch + i] = jnp.where(slot < counts[k][0], decayed, 0.0)

            loop(0, bunch, body)
        if t < ny - 1:
            fars[t, q] = remote(
                pair.at[g, q], far.at[t, q], far_send.at[t, q], far_recv.at[t, q], {"dp": ahead}
            )
            fars[t, q].start()

    gu_acc[...] = jnp.zeros_like(gu_acc)
    dh_acc[...] = jnp.zeros_like(dh_acc)
    for held in (wgs, wus, wds):
        held[0] = jnp.zeros((blk, blk), BF16)
    own_blocks(0)
    pl.semaphore_wait(barrier, len(greet))
    gather_begin(0)
    for copy in loads:
        copy.start()
    own_blocks(1)
    for copy in loads[:2]:
        copy.wait()

    def tokens_step(s):
        gather_step(0, s)

        @pl.when(s == nz - 1)
        def _():
            gather_begin(1)

        gather_work(0, s, gate_up)

    loop(0, nz + 1, tokens_step)

    for h in range(hblocks):
        gate = gu_acc[h, :, :blk]
        sig = 1.0 / (1.0 + jnp.exp(-gate))
        hidden = (gate * sig * gu_acc[h, :, blk:]).astype(BF16)
        hid[:, h * blk:(h + 1) * blk] = hidden
        hid_tiles[h] = hidden

    loads[2].wait()
    both_work(0)

    def cotangent_step(s):
        gather_step(1, s)

        @pl.when(s > 1)
        def _():
            both_step(0, s - 1)

        @pl.when(s > 0)
        def _():
            line_work(0, s, False)

        @pl.when(s == nz)
        def _():
            loop(1, nz, lambda t: line_cross(0, t))
            rx(0, z).start()

        gather_work(1, s, hidden_back)

    loop(0, nz + 1, cotangent_step)

    for h in range(hblocks):
        gate = gu_acc[h, :, :blk]
        up_part = gu_acc[h, :, blk:]
        dhid = dh_acc[h]
        sig = 1.0 / (1.0 + jnp.exp(-gate))
        act = gate * sig
        d_gate = (dhid * up_part * sig * (1.0 + gate * (1.0 - sig))).astype(BF16)
        d_up = (dhid * act).astype(BF16)
        two = jnp.concatenate([d_gate, d_up], axis=1)
        dgu[:, 2 * h * blk:2 * (h + 1) * blk] = two
        dgu_tiles[h] = two

    tasks = []
    for t in range(1, ny):
        for q in range(parts):
            tasks.append((t, q))

    def own_share(count):
        for _ in range(min(count, len(tasks))):
            t, q = tasks.pop(0)
            give(t, q)
            keep(t, q)
            if t < ny - 1:
                pair_add(t, q)

    cuts = [1 + (nz * i) // 4 for i in range(5)]

    def steps(i, fn):
        loop(cuts[i], cuts[i + 1], fn)

    def work_in(t):
        line_work(1, t, True)

    line_out = functools.partial(line_step, 0)
    line_in = functools.partial(line_step, 1)
    both_in = functools.partial(both_step, 1)

    give(0, 0)
    keep(0, 0)
    pair_add(0, 0)
    both_work(1)
    steps(0, line_out)
    steps(0, both_in)
    for q in range(1, parts):
        give(0, q)
        keep(0, q)
        steps(q - 1, work_in)
        pair_add(0, q)
        steps(q, line_out)
        steps(q, both_in)
    for i in range(parts, 4):
        steps(i, line_out)
        steps(i, both_in)
    both_final(0)
    for i in range(parts - 1, 4):
        steps(i, work_in)
    steps(0, line_in)
    own_share(1)
    line_final(0)
    both_final(1)
    steps(1, line_in)
    own_share(1)
    steps(2, line_in)
    own_share(len(tasks))
    steps(3, line_in)
    line_final(1)
    for q in range(parts):
        pair_add(ny - 1, q)
    for a in range(2):
        gather_done(a)
        scatter_done(a)
    for copy in list(pairs.values()) + list(fars.values()):
        copy.wait_send()


def layer(tokens, out_grad, wg, wu, wd, gtab, dtab, rows, cols, drows, dcols, gcount, dcount, n, nd):
    ntok, width = tokens.shape
    slots, blk, _ = wg.shape
    share = slots // nd
    ny = nd // 2
    nz = n // 2
    hblocks = HID_DEV // blk
    per = width // blk
    rxb = (cross_first(per, "ffn_out"), cross_first(per, "input_grad"))
    parts = slot_parts(share)
    bunch = share // parts
    dma = pltpu.SemaphoreType.DMA
    return pl.pallas_call(
        functools.partial(layer_kernel, n, nd, 1.0 / math.sqrt(ntok * nd)),
        out_shape=(
            pltpu.VMEM((ntok, width), BF16),
            pltpu.VMEM((ntok, width), BF16),
            pltpu.VMEM((3, share, blk, blk), F32),
        ),
        in_specs=[pl.BlockSpec(memory_space=pltpu.SMEM)] * 8
        + [pl.BlockSpec(memory_space=pl.ANY)] * 5,
        out_specs=(pl.BlockSpec(memory_space=pltpu.VMEM),) * 3,
        scratch_shapes=[
            pltpu.VMEM((n * per, ntok, blk), BF16),
            pltpu.VMEM((n * per, ntok, blk), BF16),
            pltpu.VMEM((slots + 1, blk, blk), BF16),
            pltpu.VMEM((slots + 1, blk, blk), BF16),
            pltpu.VMEM((slots + 1, blk, blk), BF16),
            pltpu.VMEM((hblocks, ntok, 2 * blk), F32),
            pltpu.VMEM((hblocks, ntok, blk), F32),
            pltpu.VMEM((ntok, hblocks * blk), BF16),
            pltpu.VMEM((ntok, 2 * hblocks * blk), BF16),
            pltpu.VMEM((hblocks, ntok, blk), BF16),
            pltpu.VMEM((hblocks, ntok, 2 * blk), BF16),
            pltpu.VMEM((n * per, ntok, blk), BF16),
            pltpu.VMEM((n * per, ntok, blk), BF16),
            *[pltpu.VMEM((nz + 1, per - xb, ntok, blk), BF16) for xb in rxb],
            *[pltpu.VMEM((nz + 1, 2 * xb, ntok, blk), BF16) for xb in rxb],
            *[pltpu.VMEM((nz, per - xb, ntok, blk), BF16) for xb in rxb],
            *[pltpu.VMEM((xb, ntok, blk), BF16) for xb in rxb],
            pltpu.VMEM((ny, 2, parts, 3, bunch, blk, blk), BF16),
            pltpu.VMEM((ny, parts, 3, bunch, blk, blk), BF16),
            pltpu.VMEM((max(ny - 1, 1), parts, 3, bunch, blk, blk), BF16),
            pltpu.VMEM((2, ntok, width), BF16),
            dma((2,)),
            dma((3,)),
            dma((2, nz)), dma((2, nz)), dma((2,)), dma((2,)),
            dma((2, 2, nz)), dma((2, nz)), dma((2, 2, nz)), dma((2, nz)),
            dma((2, nz)), dma((2, nz)), dma((2,)), dma((2,)),
            dma((2, nz)), dma((2, nz + 1)), dma((2, nz)), dma((2, nz + 1)),
            dma((ny, parts)), dma((ny, parts)), dma((ny, parts)), dma((ny, parts)),
        ],
        compiler_params=pltpu.CompilerParams(
            collective_id=0, has_side_effects=True, vmem_limit_bytes=56 << 20
        ),
    )(gtab, dtab, rows, cols, drows, dcols, gcount, dcount, tokens, out_grad, wg, wu, wd)


def slot_table(features, hidden, count, dblocks, hblocks):
    slot = jnp.arange(features.shape[0])
    key = jnp.where(slot < count[0], features * hblocks + hidden, -1)
    hit = key[None, :] == jnp.arange(dblocks * hblocks)[:, None]
    return jnp.sum(jnp.where(hit, slot[None, :] + 1, 0), axis=1).astype(jnp.int32)


def hand_over_kernel(ffn_ref, in_ref, step_ref, ffn_out, input_grad, gate_step, up_step, down_step, sems):
    copies = [
        pltpu.make_async_copy(src, dst, sems.at[k])
        for k, (src, dst) in enumerate(
            (
                (step_ref.at[0], gate_step.at[0]),
                (step_ref.at[1], up_step.at[0]),
                (step_ref.at[2], down_step.at[0]),
                (ffn_ref, ffn_out),
                (in_ref, input_grad),
            )
        )
    ]
    for copy in copies:
        copy.start()
    for copy in copies:
        copy.wait()


def hand_over(ffn, inp, steps):
    one = jax.ShapeDtypeStruct((1,) + steps.shape[1:], F32)
    return pl.pallas_call(
        hand_over_kernel,
        out_shape=(
            jax.ShapeDtypeStruct(ffn.shape, BF16),
            jax.ShapeDtypeStruct(inp.shape, BF16),
            one, one, one,
        ),
        in_specs=[pl.BlockSpec(memory_space=pl.ANY)] * 3,
        out_specs=(pl.BlockSpec(memory_space=pl.ANY),) * 5,
        scratch_shapes=[pltpu.SemaphoreType.DMA((5,))],
        compiler_params=pltpu.CompilerParams(vmem_limit_bytes=1 << 20),
    )(ffn, inp, steps)


def local(
    tokens, out_grad, w_gate, w_up, w_down, gu_rows, gu_cols, gu_count, dn_rows, dn_cols, dn_count
):
    n = lax.axis_size("mp")
    nd = lax.axis_size("dp")
    wg, wu, wd = w_gate[0], w_up[0], w_down[0]
    blk = wg.shape[-1]
    dblocks = tokens.shape[1] * n // blk
    hblocks = HID_DEV // blk
    gtab = slot_table(gu_rows[0], gu_cols[0], gu_count, dblocks, hblocks)
    dtab = slot_table(dn_cols[0], dn_rows[0], dn_count, dblocks, hblocks)
    ffn, inp, steps = layer(
        tokens, out_grad, wg, wu, wd, gtab, dtab,
        gu_rows[0], gu_cols[0], dn_rows[0], dn_cols[0], gu_count, dn_count, n, nd,
    )
    return hand_over(ffn, inp, steps)


def solution(mesh):
    in_specs = (
        P("dp", "mp"),
        P("dp", "mp"),
        P("mp", None, None, None),
        P("mp", None, None, None),
        P("mp", None, None, None),
        P("mp", None),
        P("mp", None),
        P("mp"),
        P("mp", None),
        P("mp", None),
        P("mp"),
    )
    out_specs = (
        P("dp", "mp"),
        P("dp", "mp"),
        P("mp", "dp", None, None),
        P("mp", "dp", None, None),
        P("mp", "dp", None, None),
    )
    return jax.shard_map(local, mesh=mesh, in_specs=in_specs, out_specs=out_specs, check_vma=False)
```

```python
import functools
import math

import jax
import jax.numpy as jnp
from jax import lax
from jax.experimental import pallas as pl
from jax.experimental.pallas import tpu as pltpu
from jax.sharding import PartitionSpec as P

HID_DEV = 896
MESH = pl.DeviceIdType.MESH
F32 = jnp.float32
BF16 = jnp.bfloat16

decay_coef = 8.0


def dot(left, right, contract):
    return lax.dot_general(left, right, (contract, ((), ())), preferred_element_type=F32)


def loop(lo, hi, fn):
    def body(i, carry):
        fn(i)
        return carry

    lax.fori_loop(lo, hi, body, 0)


CROSS_FIRST = {"tokens": 2, "out_grad": 3, "ffn_out": 4, "input_grad": 2}


def cross_first(per, name):
    return max(1, per * CROSS_FIRST[name] // 8)


def slot_parts(share):
    return 3 if share % 3 == 0 else 1


def layer_kernel(
    n, nd, scale_root, gtab_ref, dtab_ref, rows_ref, cols_ref, drows_ref, dcols_ref, gcount_ref, dcount_ref,
    x_ref, dy_ref, wg_ref, wu_ref, wd_ref,
    out_ref, in_ref, step_ref,
    xs, dys, wgs, wus, wds, gu_acc, dh_acc, hid, dgu, hid_tiles, dgu_tiles,
    part_o, part_i, line_o, line_i, both_o, both_i, side_o, side_i, last_o, last_i,
    grad, pair, far, stage, xs_far, dgu_far, gu_grad, gu_near,
    own_sem, w_sem,
    gx_send, gx_recv, gxx_send, gxx_recv, gl_send, gl_recv, glx_send, glx_recv,
    rx_send, rx_recv, rxx_send, rxx_recv, rl_send, rl_recv, rlx_send, rlx_recv,
    pair_send, pair_recv, far_send, far_recv, relay_send, relay_recv, dgu_sem, near_send, near_recv,
):
    blk = wg_ref.shape[-1]
    ntok, width = x_ref.shape
    per = width // blk
    hblocks = gu_acc.shape[0]
    nz = n // 2
    gxb = (cross_first(per, "tokens"), cross_first(per, "out_grad"))
    rxb = (cross_first(per, "ffn_out"), cross_first(per, "input_grad"))
    me = lax.axis_index("mp")
    z, x = me // 2, me % 2
    other = 1 - x
    across = {"mp": 2 * z + other}
    up = {"mp": 2 * ((z + 1) % nz) + x}
    down = {"mp": 2 * ((z + nz - 1) % nz) + x}
    toward = (up, down)
    has = (z < nz - 1, z > 0)
    dp = lax.axis_index("dp")
    ny = nd // 2
    y, core = dp // 2, dp % 2
    partner = 2 * y + (1 - core)
    ahead = 2 * ((y + 1) % ny) + core
    behind = 2 * ((y + ny - 1) % ny) + core

    barrier = pltpu.get_barrier_semaphore()
    greet = [across, up, down, {"dp": partner}, {"dp": ahead}]
    if ny > 2:
        greet.append({"dp": behind})
    for device in greet:
        pl.semaphore_signal(barrier, inc=1, device_id=device, device_id_type=MESH)

    full = (xs, dys)
    owns = [
        pltpu.make_async_copy(shard, stage.at[a], own_sem.at[a])
        for a, shard in enumerate((x_ref, dy_ref))
    ]
    loads = [
        pltpu.make_async_copy(w, held.at[pl.ds(1, w.shape[0])], w_sem.at[k])
        for k, (w, held) in enumerate(((wg_ref, wgs), (wu_ref, wus), (wd_ref, wds)))
    ]
    for copy in owns:
        copy.start()

    def remote(src, dst, send, recv, device):
        return pltpu.make_async_remote_copy(
            src_ref=src, dst_ref=dst, send_sem=send, recv_sem=recv,
            device_id=device, device_id_type=MESH,
        )

    def zspan(o, c, xb):
        return pl.ds((2 * o + c) * per + c * xb, per - xb)

    def bspan(o, xb):
        return pl.ds((2 * o + 1) * per - xb, 2 * xb)

    def xspan(o, c, xb):
        return pl.ds((2 * o + 1) * per - (1 - c) * xb, xb)

    def gx(a, o):
        r = full[a].at[zspan(o, x, gxb[a])]
        return remote(r, r, gx_send.at[a, o], gx_recv.at[a, o], across)

    def gxx(a):
        r = full[a].at[xspan(z, x, gxb[a])]
        return remote(r, r, gxx_send.at[a], gxx_recv.at[a], across)

    def gl(a, o, j):
        r = full[a].at[zspan(o, x, gxb[a])]
        return remote(r, r, gl_send.at[a, j, o], gl_recv.at[a, o], toward[j])

    def glx(a, o, j):
        r = full[a].at[bspan(o, gxb[a])]
        return remote(r, r, glx_send.at[a, j, o], glx_recv.at[a, o], toward[j])

    def gather_begin(a):
        for j in range(2):
            @pl.when(has[j])
            def _():
                gl(a, z, j).start()
        gx(a, z).start()
        gxx(a).start()

    def gather_step(a, s):
        for j in range(2):
            o = z - s if j == 0 else z + s

            @pl.when((s > 0) & (o >= 0) & (o < nz))
            def _():
                gl(a, o, j).wait_recv()

                @pl.when(has[j])
                def _():
                    gl(a, o, j).start()

                gx(a, o).start()

        @pl.when(s == 1)
        def _():
            gxx(a).wait_recv()
            for j in range(2):
                @pl.when(has[j])
                def _():
                    glx(a, z, j).start()

        for j in range(2):
            o = z - (s - 1) if j == 0 else z + (s - 1)

            @pl.when((s > 1) & (o >= 0) & (o < nz))
            def _():
                glx(a, o, j).wait_recv()

                @pl.when(has[j])
                def _():
                    glx(a, o, j).start()

    swap = ny == 2

    def relay(kind, o):
        span = (
            zspan(o, x, gxb[0]), zspan(o, other, gxb[0]), bspan(o, gxb[0])
        )[kind]
        return remote(
            xs.at[span], xs_far.at[span], relay_send.at[kind, o], relay_recv.at[kind, o], {"dp": ahead}
        )

    def gather_work(a, s, work):
        def side(j):
            sign = 2 * j - 1
            near = z + sign * s
            late = z + sign * (s - 1)

            @pl.when((near >= 0) & (near < nz) & ((s > 0) | (j == 0)))
            def _():
                if swap and a == 0:
                    relay(0, near).start()
                work(zspan(near, x, gxb[a]))

            @pl.when((s > 0) & (late >= 0) & (late < nz) & ((s > 1) | (j == 0)))
            def _():
                gx(a, late).wait_recv()
                if swap and a == 0:
                    relay(1, late).start()
                    relay(2, late).start()
                work(zspan(late, other, gxb[a]))
                work(bspan(late, gxb[a]))

        loop(0, 2, side)

    def gather_done(a):
        def body(o):
            gx(a, o).wait_send()
            for j in range(2):
                passed = (o <= z) if j == 0 else (o >= z)

                @pl.when(has[j] & passed)
                def _():
                    gl(a, o, j).wait_send()
                    glx(a, o, j).wait_send()

        loop(0, nz, body)
        gxx(a).wait_send()

    def own_blocks(a):
        owns[a].wait()
        for f in range(per):
            full[a][me * per + f] = stage[a, :, f * blk:(f + 1) * blk]

    def features(a, start, count):
        return jnp.concatenate([full[a][start + f] for f in range(count)], axis=1)

    def gate_up(span):
        start, count = span.start, span.size
        left = features(0, start, count)
        for h in range(hblocks):
            tabs = [gtab_ref[(start + f) * hblocks + h] for f in range(count)]
            rhs = jnp.concatenate(
                [jnp.concatenate([wgs[t], wus[t]], axis=1) for t in tabs], axis=0
            )
            gu_acc[h] += dot(left, rhs, ((1,), (0,)))

    def hidden_back(span):
        start, count = span.start, span.size
        left = features(1, start, count)
        for h in range(0, hblocks, 2):
            hs = range(h, min(h + 2, hblocks))
            rhs = jnp.concatenate(
                [
                    jnp.concatenate(
                        [wds[dtab_ref[(start + f) * hblocks + k]] for f in range(count)], axis=1
                    )
                    for k in hs
                ],
                axis=0,
            )
            got = dot(left, rhs, ((1,), (1,)))
            for i, k in enumerate(hs):
                dh_acc[k] += got[:, i * blk:(i + 1) * blk]

    part = (part_o, part_i)
    line = (line_o, line_i)
    both = (both_o, both_i)
    side_in = (side_o, side_i)
    last = (last_o, last_i)
    results = (out_ref, in_ref)

    def out_range(span):
        start, count = span.start, span.size
        for i in range(0, count, 2):
            fs = range(i, min(i + 2, count))
            rhs = jnp.concatenate(
                [
                    jnp.concatenate([wds[dtab_ref[(start + f) * hblocks + h]] for f in fs], axis=1)
                    for h in range(hblocks)
                ],
                axis=0,
            )
            got = dot(hid[...], rhs, ((1,), (0,))).astype(BF16)
            for k, f in enumerate(fs):
                part_o[start + f] = got[:, k * blk:(k + 1) * blk]

    def in_range(span):
        start, count = span.start, span.size
        for i in range(0, count, 2):
            fs = range(i, min(i + 2, count))
            rhs = jnp.concatenate(
                [
                    jnp.concatenate(
                        [
                            held[t]
                            for t in [gtab_ref[(start + f) * hblocks + h] for h in range(hblocks)]
                            for held in (wgs, wus)
                        ],
                        axis=1,
                    )
                    for f in fs
                ],
                axis=0,
            )
            got = dot(dgu[...], rhs, ((1,), (1,))).astype(BF16)
            for k, f in enumerate(fs):
                part_i[start + f] = got[:, k * blk:(k + 1) * blk]

    ranges = (out_range, in_range)

    def rx(a, o):
        return remote(
            part[a].at[zspan(o, other, rxb[a])], side_in[a].at[o],
            rx_send.at[a, o], rx_recv.at[a, o], across,
        )

    def rxx(a):
        return remote(
            part[a].at[xspan(z, other, rxb[a])], last[a],
            rxx_send.at[a], rxx_recv.at[a], across,
        )

    def place(o, j):
        if j == 0:
            return o
        return jnp.where(o == z - 1, nz, o)

    def rl(a, o, j):
        slot = place(o, j)
        return remote(
            part[a].at[zspan(o, x, rxb[a])], line[a].at[slot],
            rl_send.at[a, o], rl_recv.at[a, slot], toward[j],
        )

    def rlx(a, o, j):
        slot = place(o, j)
        return remote(
            part[a].at[bspan(o, rxb[a])], both[a].at[slot],
            rlx_send.at[a, o], rlx_recv.at[a, slot], toward[j],
        )

    def line_wait(a, slot):
        remote(
            part[a].at[pl.ds(0, per - rxb[a])], line[a].at[slot], rl_send.at[a, 0], rl_recv.at[a, slot], up
        ).wait_recv()

    def both_wait(a, slot):
        remote(
            part[a].at[pl.ds(0, 2 * rxb[a])], both[a].at[slot], rlx_send.at[a, 0], rlx_recv.at[a, slot], up
        ).wait_recv()

    def dest(t, j):
        o = nz - t + z if j == 0 else t + z - nz
        return o, (o >= 0) & (o < nz) & (t < nz)

    def both_add(a, o, slot):
        base = bspan(o, rxb[a]).start
        for i in range(2 * rxb[a]):
            part[a][base + i] = (part[a][base + i].astype(F32) + both[a][slot, i].astype(F32)).astype(BF16)

    def both_work(a):
        loop(0, nz, lambda o: ranges[a](bspan(o, rxb[a])))

    def both_step(a, t):
        for j in range(2):
            o, valid = dest(t, j)

            @pl.when(valid)
            def _():
                @pl.when(has[1 - j])
                def _():
                    both_wait(a, o)
                    both_add(a, o, o)

                rlx(a, o, j).start()

    def both_final(a):
        @pl.when(z > 0)
        def _():
            both_wait(a, z)
            both_add(a, z, z)

        @pl.when(z < nz - 1)
        def _():
            both_wait(a, nz)
            both_add(a, z, nz)

        rxx(a).start()

    def line_work(a, t, send):
        def body(j):
            o = jnp.where(j == 0, nz - t + z, t + z - nz)

            @pl.when((o >= 0) & (o < nz) & ((j == 0) | (t < nz)))
            def _():
                ranges[a](zspan(o, other, rxb[a]))
                if send:
                    rx(a, o).start()
                ranges[a](zspan(o, x, rxb[a]))

        loop(0, 2, body)

    def line_step(a, t):
        for j in range(2):
            o, valid = dest(t, j)

            @pl.when(valid)
            def _():
                rx(a, o).wait_recv()
                base = zspan(o, x, rxb[a]).start

                @pl.when(has[1 - j])
                def _():
                    line_wait(a, o)

                    for i in range(per - rxb[a]):
                        part[a][base + i] = (
                            part[a][base + i].astype(F32)
                            + side_in[a][o, i].astype(F32)
                            + line[a][o, i].astype(F32)
                        ).astype(BF16)

                @pl.when(jnp.logical_not(has[1 - j]))
                def _():
                    for i in range(per - rxb[a]):
                        part[a][base + i] = (
                            part[a][base + i].astype(F32) + side_in[a][o, i].astype(F32)
                        ).astype(BF16)

                rl(a, o, j).start()

    def line_final(a):
        rx(a, z).wait_recv()
        xb = rxb[a]
        zb = per - xb
        base = zspan(z, x, xb).start

        def lanes(i):
            return pl.ds(pl.multiple_of((x * xb + i) * blk, blk), blk)

        def finish_line(slots):
            for slot in slots:
                line_wait(a, slot)

            for i in range(zb):
                total = part[a][base + i].astype(F32) + side_in[a][z, i].astype(F32)
                for slot in slots:
                    total = total + line[a][slot, i].astype(F32)
                results[a][:, lanes(i)] = total.astype(BF16)

        @pl.when(z == 0)
        def _():
            finish_line([nz])

        @pl.when(z == nz - 1)
        def _():
            finish_line([z])

        @pl.when((z > 0) & (z < nz - 1))
        def _():
            finish_line([z, nz])

        rxx(a).wait_recv()

        for i in range(xb):
            at = pl.ds(pl.multiple_of((other * zb + i) * blk, blk), blk)
            total = part[a][xspan(z, x, xb).start + i].astype(F32) + last[a][i].astype(F32)
            results[a][:, at] = total.astype(BF16)

    def scatter_done(a):
        def body(o):
            rx(a, o).wait_send()
            for j in range(2):
                passed = (o > z) if j == 0 else (o < z)

                @pl.when(passed)
                def _():
                    rl(a, o, j).wait_send()
                    rlx(a, o, j).wait_send()

        loop(0, nz, body)
        rxx(a).wait_send()

    parts, kinds, bunch = grad.shape[2:5]

    def group(t):
        return (y + 2 * ny - 1 - t) % ny

    def slot_grads(t, c, q):
        g = group(t)
        base = (2 * g + c) * parts * bunch + q * bunch
        unit = 4

        def body(i):
            for j in range(unit):
                e = i * unit + j
                s = base + e
                down_grad = dot(hid_tiles[drows_ref[s]], dys[dcols_ref[s]], ((0,), (0,)))
                grad[g, c, q, kinds - 1, e] = down_grad.astype(BF16)
                if not swap:
                    pair_grad = dot(xs[rows_ref[s]], dgu_tiles[cols_ref[s]], ((0,), (0,)))
                    grad[g, c, q, 0, e] = pair_grad[:, :blk].astype(BF16)
                    grad[g, c, q, 1, e] = pair_grad[:, blk:].astype(BF16)

        loop(0, bunch // unit, body)

    pairs = {}
    fars = {}
    weights = (wgs, wus, wds)
    counts = (gcount_ref, gcount_ref, dcount_ref)

    def step(k, i, total):
        slot = dp * parts * bunch + i
        decayed = total * scale_root + decay_coef * weights[k][slot + 1].astype(F32)
        step_ref[k, i] = jnp.where(slot < counts[k][0], decayed, 0.0)

    if swap:
        dgu_copy = remote(dgu_tiles, dgu_far, dgu_sem.at[0], dgu_sem.at[1], {"dp": ahead})

    def near_copy(q):
        return remote(
            gu_grad.at[1 - core, q], gu_near.at[q], near_send.at[q], near_recv.at[q], {"dp": partner}
        )

    def both_groups(c, q):
        base = (2 * y + c) * parts * bunch + q * bunch
        unit = 4

        def body(i):
            for j in range(unit):
                e = i * unit + j
                r, h = rows_ref[base + e], cols_ref[base + e]
                total = dot(xs[r], dgu_tiles[h], ((0,), (0,)))
                total = total + dot(xs_far[r], dgu_far[h], ((0,), (0,)))
                gu_grad[c, q, 0, e] = total[:, :blk].astype(BF16)
                gu_grad[c, q, 1, e] = total[:, blk:].astype(BF16)

        loop(0, bunch // unit, body)

    def swap_wait():
        dgu_copy.wait_recv()

        def body(o):
            for kind in range(3):
                relay(kind, o).wait_recv()

        loop(0, nz, body)

    def swap_work(q):
        both_groups(1 - core, q)
        near_copy(q).start()
        both_groups(core, q)

    def swap_add(q):
        near_copy(q).wait_recv()
        for k in range(2):
            loop(
                0, bunch,
                lambda i: step(
                    k, q * bunch + i, gu_grad[core, q, k, i].astype(F32) + gu_near[q, k, i].astype(F32)
                ),
            )

    def swap_done():
        dgu_copy.wait_send()

        def body(o):
            for kind in range(3):
                relay(kind, o).wait_send()

        loop(0, nz, body)
        for q in range(parts):
            near_copy(q).wait_send()

    def give(t, q):
        slot_grads(t, 1 - core, q)
        g = group(t)
        pairs[t, q] = remote(
            grad.at[g, 1 - core, q], pair.at[g, q],
            pair_send.at[t, q], pair_recv.at[t, q], {"dp": partner},
        )
        pairs[t, q].start()

    def keep(t, q):
        slot_grads(t, core, q)

    def pair_add(t, q):
        g = group(t)
        pairs[t, q].wait_recv()
        if t > 0:
            fars[t - 1, q].wait_recv()
        for k in range(kinds):
            def body(i):
                total = pair[g, q, k, i].astype(F32) + grad[g, core, q, k, i].astype(F32)
                if t > 0:
                    total = total + far[t - 1, q, k, i].astype(F32)
                if t < ny - 1:
                    pair[g, q, k, i] = total.astype(BF16)
                else:
                    step(3 - kinds + k, q * bunch + i, total)

            loop(0, bunch, body)
        if t < ny - 1:
            fars[t, q] = remote(
                pair.at[g, q], far.at[t, q], far_send.at[t, q], far_recv.at[t, q], {"dp": ahead}
            )
            fars[t, q].start()

    gu_acc[...] = jnp.zeros_like(gu_acc)
    dh_acc[...] = jnp.zeros_like(dh_acc)
    for held in (wgs, wus, wds):
        held[0] = jnp.zeros((blk, blk), BF16)
    own_blocks(0)
    pl.semaphore_wait(barrier, len(greet))
    gather_begin(0)
    for copy in loads:
        copy.start()
    own_blocks(1)
    for copy in loads[:2]:
        copy.wait()

    def tokens_step(s):
        gather_step(0, s)

        @pl.when(s == nz - 1)
        def _():
            gather_begin(1)

        gather_work(0, s, gate_up)

    loop(0, nz + 1, tokens_step)

    for h in range(hblocks):
        gate = gu_acc[h, :, :blk]
        sig = 1.0 / (1.0 + jnp.exp(-gate))
        hidden = (gate * sig * gu_acc[h, :, blk:]).astype(BF16)
        hid[:, h * blk:(h + 1) * blk] = hidden
        hid_tiles[h] = hidden

    loads[2].wait()
    both_work(0)

    def cotangent_step(s):
        gather_step(1, s)

        @pl.when(s > 0)
        def _():
            both_step(0, s)
            line_work(0, s, True)

        gather_work(1, s, hidden_back)

        @pl.when(s > 1)
        def _():
            line_step(0, s - 1)

    loop(0, nz + 1, cotangent_step)

    for h in range(hblocks):
        gate = gu_acc[h, :, :blk]
        up_part = gu_acc[h, :, blk:]
        dhid = dh_acc[h]
        sig = 1.0 / (1.0 + jnp.exp(-gate))
        act = gate * sig
        d_gate = (dhid * up_part * sig * (1.0 + gate * (1.0 - sig))).astype(BF16)
        d_up = (dhid * act).astype(BF16)
        two = jnp.concatenate([d_gate, d_up], axis=1)
        dgu[:, 2 * h * blk:2 * (h + 1) * blk] = two
        dgu_tiles[h] = two

    tasks = []
    for t in range(1, ny):
        for q in range(parts):
            tasks.append((t, q))

    def own_share(count):
        for _ in range(min(count, len(tasks))):
            t, q = tasks.pop(0)
            give(t, q)
            keep(t, q)
            if t < ny - 1:
                pair_add(t, q)

    cuts = [1 + (nz * i) // 4 for i in range(5)]

    def steps(i, fn):
        loop(cuts[i], cuts[i + 1], fn)

    def work_in(t):
        line_work(1, t, True)

    line_in = functools.partial(line_step, 1)
    both_in = functools.partial(both_step, 1)

    if swap:
        dgu_copy.start()
    both_work(1)
    give(0, 0)
    keep(0, 0)
    pair_add(0, 0)
    both_final(0)
    steps(0, both_in)
    for q in range(1, parts):
        give(0, q)
        keep(0, q)
        steps(q - 1, work_in)
        pair_add(0, q)
        steps(q, both_in)
    for i in range(parts, 4):
        steps(i, both_in)
    for i in range(parts - 1, 4):
        steps(i, work_in)
    steps(0, line_in)
    if not swap:
        own_share(1)
    line_final(0)
    steps(1, line_in)
    both_final(1)
    if swap:
        swap_wait()
        swap_work(0)
    else:
        own_share(1)
    steps(2, line_in)
    if swap:
        for q in range(1, parts):
            swap_work(q)
    own_share(len(tasks))
    steps(3, line_in)
    if swap:
        for q in range(parts):
            swap_add(q)
    line_final(1)
    for q in range(parts):
        pair_add(ny - 1, q)
    if swap:
        swap_done()
    for a in range(2):
        gather_done(a)
        scatter_done(a)
    for copy in list(pairs.values()) + list(fars.values()):
        copy.wait_send()


def layer(tokens, out_grad, wg, wu, wd, gtab, dtab, rows, cols, drows, dcols, gcount, dcount, n, nd):
    ntok, width = tokens.shape
    slots, blk, _ = wg.shape
    share = slots // nd
    ny = nd // 2
    nz = n // 2
    hblocks = HID_DEV // blk
    per = width // blk
    rxb = (cross_first(per, "ffn_out"), cross_first(per, "input_grad"))
    parts = slot_parts(share)
    bunch = share // parts
    swap = ny == 2
    kinds = 1 if swap else 3
    dma = pltpu.SemaphoreType.DMA
    return pl.pallas_call(
        functools.partial(layer_kernel, n, nd, 1.0 / math.sqrt(ntok * nd)),
        out_shape=(
            pltpu.VMEM((ntok, width), BF16),
            pltpu.VMEM((ntok, width), BF16),
            pltpu.VMEM((3, share, blk, blk), F32),
        ),
        in_specs=[pl.BlockSpec(memory_space=pltpu.SMEM)] * 8
        + [pl.BlockSpec(memory_space=pl.ANY)] * 5,
        out_specs=(pl.BlockSpec(memory_space=pltpu.VMEM),) * 3,
        scratch_shapes=[
            pltpu.VMEM((n * per, ntok, blk), BF16),
            pltpu.VMEM((n * per, ntok, blk), BF16),
            pltpu.VMEM((slots + 1, blk, blk), BF16),
            pltpu.VMEM((slots + 1, blk, blk), BF16),
            pltpu.VMEM((slots + 1, blk, blk), BF16),
            pltpu.VMEM((hblocks, ntok, 2 * blk), F32),
            pltpu.VMEM((hblocks, ntok, blk), F32),
            pltpu.VMEM((ntok, hblocks * blk), BF16),
            pltpu.VMEM((ntok, 2 * hblocks * blk), BF16),
            pltpu.VMEM((hblocks, ntok, blk), BF16),
            pltpu.VMEM((hblocks, ntok, 2 * blk), BF16),
            pltpu.VMEM((n * per, ntok, blk), BF16),
            pltpu.VMEM((n * per, ntok, blk), BF16),
            *[pltpu.VMEM((nz + 1, per - xb, ntok, blk), BF16) for xb in rxb],
            *[pltpu.VMEM((nz + 1, 2 * xb, ntok, blk), BF16) for xb in rxb],
            *[pltpu.VMEM((nz, per - xb, ntok, blk), BF16) for xb in rxb],
            *[pltpu.VMEM((xb, ntok, blk), BF16) for xb in rxb],
            pltpu.VMEM((ny, 2, parts, kinds, bunch, blk, blk), BF16),
            pltpu.VMEM((ny, parts, kinds, bunch, blk, blk), BF16),
            pltpu.VMEM((max(ny - 1, 1), parts, kinds, bunch, blk, blk), BF16),
            pltpu.VMEM((2, ntok, width), BF16),
            pltpu.VMEM((n * per if swap else 1, ntok, blk), BF16),
            pltpu.VMEM((hblocks if swap else 1, ntok, 2 * blk), BF16),
            pltpu.VMEM((2, parts, 2, bunch, blk, blk) if swap else (1, 1, 1, 1, blk, blk), BF16),
            pltpu.VMEM((parts, 2, bunch, blk, blk) if swap else (1, 1, 1, blk, blk), BF16),
            dma((2,)),
            dma((3,)),
            dma((2, nz)), dma((2, nz)), dma((2,)), dma((2,)),
            dma((2, 2, nz)), dma((2, nz)), dma((2, 2, nz)), dma((2, nz)),
            dma((2, nz)), dma((2, nz)), dma((2,)), dma((2,)),
            dma((2, nz)), dma((2, nz + 1)), dma((2, nz)), dma((2, nz + 1)),
            dma((ny, parts)), dma((ny, parts)), dma((ny, parts)), dma((ny, parts)),
            dma((3, nz)), dma((3, nz)), dma((2,)), dma((parts,)), dma((parts,)),
        ],
        compiler_params=pltpu.CompilerParams(
            collective_id=0, has_side_effects=True, vmem_limit_bytes=56 << 20
        ),
    )(gtab, dtab, rows, cols, drows, dcols, gcount, dcount, tokens, out_grad, wg, wu, wd)


def slot_table(features, hidden, count, dblocks, hblocks):
    slot = jnp.arange(features.shape[0])
    key = jnp.where(slot < count[0], features * hblocks + hidden, -1)
    hit = key[None, :] == jnp.arange(dblocks * hblocks)[:, None]
    return jnp.sum(jnp.where(hit, slot[None, :] + 1, 0), axis=1).astype(jnp.int32)


def hand_over_kernel(ffn_ref, in_ref, step_ref, ffn_out, input_grad, gate_step, up_step, down_step, sems):
    copies = [
        pltpu.make_async_copy(src, dst, sems.at[k])
        for k, (src, dst) in enumerate(
            (
                (step_ref.at[0], gate_step.at[0]),
                (step_ref.at[1], up_step.at[0]),
                (step_ref.at[2], down_step.at[0]),
                (ffn_ref, ffn_out),
                (in_ref, input_grad),
            )
        )
    ]
    for copy in copies:
        copy.start()
    for copy in copies:
        copy.wait()


def hand_over(ffn, inp, steps):
    one = jax.ShapeDtypeStruct((1,) + steps.shape[1:], F32)
    return pl.pallas_call(
        hand_over_kernel,
        out_shape=(
            jax.ShapeDtypeStruct(ffn.shape, BF16),
            jax.ShapeDtypeStruct(inp.shape, BF16),
            one, one, one,
        ),
        in_specs=[pl.BlockSpec(memory_space=pl.ANY)] * 3,
        out_specs=(pl.BlockSpec(memory_space=pl.ANY),) * 5,
        scratch_shapes=[pltpu.SemaphoreType.DMA((5,))],
        compiler_params=pltpu.CompilerParams(vmem_limit_bytes=1 << 20),
    )(ffn, inp, steps)


def local(
    tokens, out_grad, w_gate, w_up, w_down, gu_rows, gu_cols, gu_count, dn_rows, dn_cols, dn_count
):
    n = lax.axis_size("mp")
    nd = lax.axis_size("dp")
    wg, wu, wd = w_gate[0], w_up[0], w_down[0]
    blk = wg.shape[-1]
    dblocks = tokens.shape[1] * n // blk
    hblocks = HID_DEV // blk
    gtab = slot_table(gu_rows[0], gu_cols[0], gu_count, dblocks, hblocks)
    dtab = slot_table(dn_cols[0], dn_rows[0], dn_count, dblocks, hblocks)
    ffn, inp, steps = layer(
        tokens, out_grad, wg, wu, wd, gtab, dtab,
        gu_rows[0], gu_cols[0], dn_rows[0], dn_cols[0], gu_count, dn_count, n, nd,
    )
    return hand_over(ffn, inp, steps)


def solution(mesh):
    in_specs = (
        P("dp", "mp"),
        P("dp", "mp"),
        P("mp", None, None, None),
        P("mp", None, None, None),
        P("mp", None, None, None),
        P("mp", None),
        P("mp", None),
        P("mp"),
        P("mp", None),
        P("mp", None),
        P("mp"),
    )
    out_specs = (
        P("dp", "mp"),
        P("dp", "mp"),
        P("mp", "dp", None, None),
        P("mp", "dp", None, None),
        P("mp", "dp", None, None),
    )
    return jax.shard_map(local, mesh=mesh, in_specs=in_specs, out_specs=out_specs, check_vma=False)
```

```python
import functools
import math

import jax
import jax.numpy as jnp
from jax import lax
from jax.experimental import pallas as pl
from jax.experimental.pallas import tpu as pltpu
from jax.sharding import PartitionSpec as P

HID_DEV = 896
MESH = pl.DeviceIdType.MESH
F32 = jnp.float32
BF16 = jnp.bfloat16

decay_coef = 8.0


def dot(left, right, contract):
    return lax.dot_general(left, right, (contract, ((), ())), preferred_element_type=F32)


def loop(lo, hi, fn):
    def body(i, carry):
        fn(i)
        return carry

    lax.fori_loop(lo, hi, body, 0)


CROSS_FIRST = {"tokens": 2, "out_grad": 3, "ffn_out": 4, "input_grad": 2}


def cross_first(per, name):
    return max(1, per * CROSS_FIRST[name] // 8)


def slot_parts(share):
    return 3 if share % 3 == 0 else 1


def layer_kernel(
    n, nd, scale_root, gtab_ref, dtab_ref, rows_ref, cols_ref, drows_ref, dcols_ref, gcount_ref, dcount_ref,
    x_ref, dy_ref, wg_ref, wu_ref, wd_ref,
    out_ref, in_ref, step_ref,
    xs, dys, wgs, wus, wds, gu_acc, dh_acc, hid, dgu, hid_tiles, dgu_tiles,
    part_o, part_i, line_o, line_i, both_o, both_i, side_o, side_i, last_o, last_i,
    grad, pair, far, stage, xs_far, dgu_far, gu_grad, gu_near,
    own_sem, w_sem,
    gx_send, gx_recv, gxx_send, gxx_recv, gl_send, gl_recv, glx_send, glx_recv,
    rx_send, rx_recv, rxx_send, rxx_recv, rl_send, rl_recv, rlx_send, rlx_recv,
    pair_send, pair_recv, far_send, far_recv, relay_send, relay_recv, dgu_sem, near_send, near_recv,
):
    blk = wg_ref.shape[-1]
    ntok, width = x_ref.shape
    per = width // blk
    hblocks = gu_acc.shape[0]
    nz = n // 2
    gxb = (cross_first(per, "tokens"), cross_first(per, "out_grad"))
    rxb = (cross_first(per, "ffn_out"), cross_first(per, "input_grad"))
    me = lax.axis_index("mp")
    z, x = me // 2, me % 2
    other = 1 - x
    across = {"mp": 2 * z + other}
    up = {"mp": 2 * ((z + 1) % nz) + x}
    down = {"mp": 2 * ((z + nz - 1) % nz) + x}
    toward = (up, down)
    has = (z < nz - 1, z > 0)
    dp = lax.axis_index("dp")
    ny = nd // 2
    y, core = dp // 2, dp % 2
    partner = 2 * y + (1 - core)
    ahead = 2 * ((y + 1) % ny) + core
    behind = 2 * ((y + ny - 1) % ny) + core

    barrier = pltpu.get_barrier_semaphore()
    greet = [across, up, down, {"dp": partner}, {"dp": ahead}]
    if ny > 2:
        greet.append({"dp": behind})
    for device in greet:
        pl.semaphore_signal(barrier, inc=1, device_id=device, device_id_type=MESH)

    full = (xs, dys)
    owns = [
        pltpu.make_async_copy(shard, stage.at[a], own_sem.at[a])
        for a, shard in enumerate((x_ref, dy_ref))
    ]
    loads = [
        pltpu.make_async_copy(w, held.at[pl.ds(1, w.shape[0])], w_sem.at[k])
        for k, (w, held) in enumerate(((wg_ref, wgs), (wu_ref, wus), (wd_ref, wds)))
    ]
    for copy in owns:
        copy.start()

    def remote(src, dst, send, recv, device):
        return pltpu.make_async_remote_copy(
            src_ref=src, dst_ref=dst, send_sem=send, recv_sem=recv,
            device_id=device, device_id_type=MESH,
        )

    def zspan(o, c, xb):
        return pl.ds((2 * o + c) * per + c * xb, per - xb)

    def bspan(o, xb):
        return pl.ds((2 * o + 1) * per - xb, 2 * xb)

    def xspan(o, c, xb):
        return pl.ds((2 * o + 1) * per - (1 - c) * xb, xb)

    def gx(a, o):
        r = full[a].at[zspan(o, x, gxb[a])]
        return remote(r, r, gx_send.at[a, o], gx_recv.at[a, o], across)

    def gxx(a):
        r = full[a].at[xspan(z, x, gxb[a])]
        return remote(r, r, gxx_send.at[a], gxx_recv.at[a], across)

    def gl(a, o, j):
        r = full[a].at[zspan(o, x, gxb[a])]
        return remote(r, r, gl_send.at[a, j, o], gl_recv.at[a, o], toward[j])

    def glx(a, o, j):
        r = full[a].at[bspan(o, gxb[a])]
        return remote(r, r, glx_send.at[a, j, o], glx_recv.at[a, o], toward[j])

    def gather_begin(a):
        for j in range(2):
            @pl.when(has[j])
            def _():
                gl(a, z, j).start()
        gx(a, z).start()
        gxx(a).start()

    def gather_step(a, s):
        for j in range(2):
            o = z - s if j == 0 else z + s

            @pl.when((s > 0) & (o >= 0) & (o < nz))
            def _():
                gl(a, o, j).wait_recv()

                @pl.when(has[j])
                def _():
                    gl(a, o, j).start()

                gx(a, o).start()

        @pl.when(s == 1)
        def _():
            gxx(a).wait_recv()
            for j in range(2):
                @pl.when(has[j])
                def _():
                    glx(a, z, j).start()

        for j in range(2):
            o = z - (s - 1) if j == 0 else z + (s - 1)

            @pl.when((s > 1) & (o >= 0) & (o < nz))
            def _():
                glx(a, o, j).wait_recv()

                @pl.when(has[j])
                def _():
                    glx(a, o, j).start()

    swap = ny == 2

    def relay(kind, o):
        span = (
            zspan(o, x, gxb[0]), zspan(o, other, gxb[0]), bspan(o, gxb[0])
        )[kind]
        return remote(
            xs.at[span], xs_far.at[span], relay_send.at[kind, o], relay_recv.at[kind, o], {"dp": ahead}
        )

    def gather_work(a, s, work):
        def side(j):
            sign = 2 * j - 1
            near = z + sign * s
            late = z + sign * (s - 1)

            @pl.when((near >= 0) & (near < nz) & ((s > 0) | (j == 0)))
            def _():
                if swap and a == 0:
                    relay(0, near).start()
                work(zspan(near, x, gxb[a]))

            @pl.when((s > 0) & (late >= 0) & (late < nz) & ((s > 1) | (j == 0)))
            def _():
                gx(a, late).wait_recv()
                if swap and a == 0:
                    relay(1, late).start()
                    relay(2, late).start()
                work(zspan(late, other, gxb[a]))
                work(bspan(late, gxb[a]))

        loop(0, 2, side)

    def gather_done(a):
        def body(o):
            gx(a, o).wait_send()
            for j in range(2):
                passed = (o <= z) if j == 0 else (o >= z)

                @pl.when(has[j] & passed)
                def _():
                    gl(a, o, j).wait_send()
                    glx(a, o, j).wait_send()

        loop(0, nz, body)
        gxx(a).wait_send()

    def own_blocks(a):
        owns[a].wait()
        for f in range(per):
            full[a][me * per + f] = stage[a, :, f * blk:(f + 1) * blk]

    def features(a, start, count):
        return jnp.concatenate([full[a][start + f] for f in range(count)], axis=1)

    def gate_up(span):
        start, count = span.start, span.size
        left = features(0, start, count)
        for h in range(hblocks):
            tabs = [gtab_ref[(start + f) * hblocks + h] for f in range(count)]
            rhs = jnp.concatenate(
                [jnp.concatenate([wgs[t], wus[t]], axis=1) for t in tabs], axis=0
            )
            gu_acc[h] += dot(left, rhs, ((1,), (0,)))

    def hidden_back(span):
        start, count = span.start, span.size
        left = features(1, start, count)
        for h in range(0, hblocks, 2):
            hs = range(h, min(h + 2, hblocks))
            rhs = jnp.concatenate(
                [
                    jnp.concatenate(
                        [wds[dtab_ref[(start + f) * hblocks + k]] for f in range(count)], axis=1
                    )
                    for k in hs
                ],
                axis=0,
            )
            got = dot(left, rhs, ((1,), (1,)))
            for i, k in enumerate(hs):
                dh_acc[k] += got[:, i * blk:(i + 1) * blk]

    part = (part_o, part_i)
    line = (line_o, line_i)
    both = (both_o, both_i)
    side_in = (side_o, side_i)
    last = (last_o, last_i)
    results = (out_ref, in_ref)

    def out_range(span):
        start, count = span.start, span.size
        for i in range(0, count, 2):
            fs = range(i, min(i + 2, count))
            rhs = jnp.concatenate(
                [
                    jnp.concatenate([wds[dtab_ref[(start + f) * hblocks + h]] for f in fs], axis=1)
                    for h in range(hblocks)
                ],
                axis=0,
            )
            got = dot(hid[...], rhs, ((1,), (0,))).astype(BF16)
            for k, f in enumerate(fs):
                part_o[start + f] = got[:, k * blk:(k + 1) * blk]

    def in_range(span):
        start, count = span.start, span.size
        for i in range(0, count, 2):
            fs = range(i, min(i + 2, count))
            rhs = jnp.concatenate(
                [
                    jnp.concatenate(
                        [
                            held[t]
                            for t in [gtab_ref[(start + f) * hblocks + h] for h in range(hblocks)]
                            for held in (wgs, wus)
                        ],
                        axis=1,
                    )
                    for f in fs
                ],
                axis=0,
            )
            got = dot(dgu[...], rhs, ((1,), (1,))).astype(BF16)
            for k, f in enumerate(fs):
                part_i[start + f] = got[:, k * blk:(k + 1) * blk]

    ranges = (out_range, in_range)

    def rx(a, o):
        return remote(
            part[a].at[zspan(o, other, rxb[a])], side_in[a].at[o],
            rx_send.at[a, o], rx_recv.at[a, o], across,
        )

    def rxx(a):
        return remote(
            part[a].at[xspan(z, other, rxb[a])], last[a],
            rxx_send.at[a], rxx_recv.at[a], across,
        )

    def place(o, j):
        if j == 0:
            return o
        return jnp.where(o == z - 1, nz, o)

    def rl(a, o, j):
        slot = place(o, j)
        return remote(
            part[a].at[zspan(o, x, rxb[a])], line[a].at[slot],
            rl_send.at[a, o], rl_recv.at[a, slot], toward[j],
        )

    def rlx(a, o, j):
        slot = place(o, j)
        return remote(
            part[a].at[bspan(o, rxb[a])], both[a].at[slot],
            rlx_send.at[a, o], rlx_recv.at[a, slot], toward[j],
        )

    def line_wait(a, slot):
        remote(
            part[a].at[pl.ds(0, per - rxb[a])], line[a].at[slot], rl_send.at[a, 0], rl_recv.at[a, slot], up
        ).wait_recv()

    def both_wait(a, slot):
        remote(
            part[a].at[pl.ds(0, 2 * rxb[a])], both[a].at[slot], rlx_send.at[a, 0], rlx_recv.at[a, slot], up
        ).wait_recv()

    def dest(t, j):
        o = nz - t + z if j == 0 else t + z - nz
        return o, (o >= 0) & (o < nz) & (t < nz)

    def both_add(a, o, slot):
        base = bspan(o, rxb[a]).start
        for i in range(2 * rxb[a]):
            part[a][base + i] = (part[a][base + i].astype(F32) + both[a][slot, i].astype(F32)).astype(BF16)

    def both_work(a):
        loop(0, nz, lambda o: ranges[a](bspan(o, rxb[a])))

    def both_step(a, t):
        for j in range(2):
            o, valid = dest(t, j)

            @pl.when(valid)
            def _():
                @pl.when(has[1 - j])
                def _():
                    both_wait(a, o)
                    both_add(a, o, o)

                rlx(a, o, j).start()

    def both_final(a):
        @pl.when(z > 0)
        def _():
            both_wait(a, z)
            both_add(a, z, z)

        @pl.when(z < nz - 1)
        def _():
            both_wait(a, nz)
            both_add(a, z, nz)

        rxx(a).start()

    def line_work(a, t, send):
        def body(j):
            o = jnp.where(j == 0, nz - t + z, t + z - nz)

            @pl.when((o >= 0) & (o < nz) & ((j == 0) | (t < nz)))
            def _():
                ranges[a](zspan(o, other, rxb[a]))
                if send:
                    rx(a, o).start()
                ranges[a](zspan(o, x, rxb[a]))

        loop(0, 2, body)

    def line_step(a, t):
        for j in range(2):
            o, valid = dest(t, j)

            @pl.when(valid)
            def _():
                rx(a, o).wait_recv()
                base = zspan(o, x, rxb[a]).start

                @pl.when(has[1 - j])
                def _():
                    line_wait(a, o)

                    for i in range(per - rxb[a]):
                        part[a][base + i] = (
                            part[a][base + i].astype(F32)
                            + side_in[a][o, i].astype(F32)
                            + line[a][o, i].astype(F32)
                        ).astype(BF16)

                @pl.when(jnp.logical_not(has[1 - j]))
                def _():
                    for i in range(per - rxb[a]):
                        part[a][base + i] = (
                            part[a][base + i].astype(F32) + side_in[a][o, i].astype(F32)
                        ).astype(BF16)

                rl(a, o, j).start()

    def line_final(a):
        rx(a, z).wait_recv()
        xb = rxb[a]
        zb = per - xb
        base = zspan(z, x, xb).start

        def lanes(i):
            return pl.ds(pl.multiple_of((x * xb + i) * blk, blk), blk)

        def finish_line(slots):
            for slot in slots:
                line_wait(a, slot)

            for i in range(zb):
                total = part[a][base + i].astype(F32) + side_in[a][z, i].astype(F32)
                for slot in slots:
                    total = total + line[a][slot, i].astype(F32)
                results[a][:, lanes(i)] = total.astype(BF16)

        @pl.when(z == 0)
        def _():
            finish_line([nz])

        @pl.when(z == nz - 1)
        def _():
            finish_line([z])

        @pl.when((z > 0) & (z < nz - 1))
        def _():
            finish_line([z, nz])

        rxx(a).wait_recv()

        for i in range(xb):
            at = pl.ds(pl.multiple_of((other * zb + i) * blk, blk), blk)
            total = part[a][xspan(z, x, xb).start + i].astype(F32) + last[a][i].astype(F32)
            results[a][:, at] = total.astype(BF16)

    def scatter_done(a):
        def body(o):
            rx(a, o).wait_send()
            for j in range(2):
                passed = (o > z) if j == 0 else (o < z)

                @pl.when(passed)
                def _():
                    rl(a, o, j).wait_send()
                    rlx(a, o, j).wait_send()

        loop(0, nz, body)
        rxx(a).wait_send()

    parts, kinds, bunch = grad.shape[2:5]

    def group(t):
        return (y + 2 * ny - 1 - t) % ny

    def slot_grads(t, c, q):
        g = group(t)
        base = (2 * g + c) * parts * bunch + q * bunch
        unit = 4

        def body(i):
            for j in range(unit):
                e = i * unit + j
                s = base + e
                down_grad = dot(hid_tiles[drows_ref[s]], dys[dcols_ref[s]], ((0,), (0,)))
                grad[g, c, q, kinds - 1, e] = down_grad.astype(BF16)
                if not swap:
                    pair_grad = dot(xs[rows_ref[s]], dgu_tiles[cols_ref[s]], ((0,), (0,)))
                    grad[g, c, q, 0, e] = pair_grad[:, :blk].astype(BF16)
                    grad[g, c, q, 1, e] = pair_grad[:, blk:].astype(BF16)

        loop(0, bunch // unit, body)

    pairs = {}
    fars = {}
    weights = (wgs, wus, wds)
    counts = (gcount_ref, gcount_ref, dcount_ref)

    def step(k, i, total):
        slot = dp * parts * bunch + i
        decayed = total * scale_root + decay_coef * weights[k][slot + 1].astype(F32)
        step_ref[k, i] = jnp.where(slot < counts[k][0], decayed, 0.0)

    if swap:
        dgu_copy = remote(dgu_tiles, dgu_far, dgu_sem.at[0], dgu_sem.at[1], {"dp": ahead})

    def near_copy(q):
        return remote(
            gu_grad.at[1 - core, q], gu_near.at[q], near_send.at[q], near_recv.at[q], {"dp": partner}
        )

    def both_groups(c, q):
        base = (2 * y + c) * parts * bunch + q * bunch
        unit = 4

        def body(i):
            for j in range(unit):
                e = i * unit + j
                r, h = rows_ref[base + e], cols_ref[base + e]
                total = dot(xs[r], dgu_tiles[h], ((0,), (0,)))
                total = total + dot(xs_far[r], dgu_far[h], ((0,), (0,)))
                gu_grad[c, q, 0, e] = total[:, :blk].astype(BF16)
                gu_grad[c, q, 1, e] = total[:, blk:].astype(BF16)

        loop(0, bunch // unit, body)

    def swap_wait():
        dgu_copy.wait_recv()

        def body(o):
            for kind in range(3):
                relay(kind, o).wait_recv()

        loop(0, nz, body)

    def swap_work(q):
        both_groups(1 - core, q)
        near_copy(q).start()
        both_groups(core, q)

    def swap_add(q):
        near_copy(q).wait_recv()
        for k in range(2):
            loop(
                0, bunch,
                lambda i: step(
                    k, q * bunch + i, gu_grad[core, q, k, i].astype(F32) + gu_near[q, k, i].astype(F32)
                ),
            )

    def swap_done():
        dgu_copy.wait_send()

        def body(o):
            for kind in range(3):
                relay(kind, o).wait_send()

        loop(0, nz, body)
        for q in range(parts):
            near_copy(q).wait_send()

    def give(t, q):
        slot_grads(t, 1 - core, q)
        g = group(t)
        pairs[t, q] = remote(
            grad.at[g, 1 - core, q], pair.at[g, q],
            pair_send.at[t, q], pair_recv.at[t, q], {"dp": partner},
        )
        pairs[t, q].start()

    def keep(t, q):
        slot_grads(t, core, q)

    def pair_add(t, q):
        g = group(t)
        pairs[t, q].wait_recv()
        if t > 0:
            fars[t - 1, q].wait_recv()
        for k in range(kinds):
            def body(i):
                total = pair[g, q, k, i].astype(F32) + grad[g, core, q, k, i].astype(F32)
                if t > 0:
                    total = total + far[t - 1, q, k, i].astype(F32)
                if t < ny - 1:
                    pair[g, q, k, i] = total.astype(BF16)
                else:
                    step(3 - kinds + k, q * bunch + i, total)

            loop(0, bunch, body)
        if t < ny - 1:
            fars[t, q] = remote(
                pair.at[g, q], far.at[t, q], far_send.at[t, q], far_recv.at[t, q], {"dp": ahead}
            )
            fars[t, q].start()

    gu_acc[...] = jnp.zeros_like(gu_acc)
    dh_acc[...] = jnp.zeros_like(dh_acc)
    for held in (wgs, wus, wds):
        held[0] = jnp.zeros((blk, blk), BF16)
    own_blocks(0)
    pl.semaphore_wait(barrier, len(greet))
    gather_begin(0)
    for copy in loads:
        copy.start()
    own_blocks(1)
    for copy in loads[:2]:
        copy.wait()

    def tokens_step(s):
        gather_step(0, s)

        @pl.when(s == nz - 1)
        def _():
            gather_begin(1)

        gather_work(0, s, gate_up)

    loop(0, nz + 1, tokens_step)

    for h in range(hblocks):
        gate = gu_acc[h, :, :blk]
        sig = 1.0 / (1.0 + jnp.exp(-gate))
        hidden = (gate * sig * gu_acc[h, :, blk:]).astype(BF16)
        hid[:, h * blk:(h + 1) * blk] = hidden
        hid_tiles[h] = hidden

    loads[2].wait()
    both_work(0)

    def cotangent_step(s):
        gather_step(1, s)

        @pl.when(s > 0)
        def _():
            both_step(0, s)
            line_work(0, s, True)

        gather_work(1, s, hidden_back)

        @pl.when((s > 1) & (s < nz))
        def _():
            line_step(0, s - 1)

    loop(0, nz + 1, cotangent_step)

    for h in range(hblocks):
        gate = gu_acc[h, :, :blk]
        up_part = gu_acc[h, :, blk:]
        dhid = dh_acc[h]
        sig = 1.0 / (1.0 + jnp.exp(-gate))
        act = gate * sig
        d_gate = (dhid * up_part * sig * (1.0 + gate * (1.0 - sig))).astype(BF16)
        d_up = (dhid * act).astype(BF16)
        two = jnp.concatenate([d_gate, d_up], axis=1)
        dgu[:, 2 * h * blk:2 * (h + 1) * blk] = two
        dgu_tiles[h] = two

    tasks = []
    for t in range(1, ny):
        for q in range(parts):
            tasks.append((t, q))

    def own_share(count):
        for _ in range(min(count, len(tasks))):
            t, q = tasks.pop(0)
            give(t, q)
            keep(t, q)
            if t < ny - 1:
                pair_add(t, q)

    cuts = [1 + (nz * i) // 4 for i in range(5)]

    def steps(i, fn):
        loop(cuts[i], cuts[i + 1], fn)

    def work_in(t):
        line_work(1, t, True)

    line_in = functools.partial(line_step, 1)
    both_in = functools.partial(both_step, 1)

    if swap:
        dgu_copy.start()
    both_work(1)
    steps(0, both_in)
    steps(0, work_in)
    give(0, 0)
    keep(0, 0)
    pair_add(0, 0)
    line_step(0, nz - 1)
    both_final(0)
    for q in range(1, parts):
        give(0, q)
        keep(0, q)
        steps(q, work_in)
        pair_add(0, q)
        steps(q, both_in)
    for i in range(parts, 4):
        steps(i, both_in)
    for i in range(parts, 4):
        steps(i, work_in)
    steps(0, line_in)
    if not swap:
        own_share(1)
    line_final(0)
    steps(1, line_in)
    both_final(1)
    if swap:
        swap_wait()
        swap_work(0)
    else:
        own_share(1)
    steps(2, line_in)
    if swap:
        for q in range(1, parts):
            swap_work(q)
    own_share(len(tasks))
    steps(3, line_in)
    if swap:
        for q in range(parts):
            swap_add(q)
    line_final(1)
    for q in range(parts):
        pair_add(ny - 1, q)
    if swap:
        swap_done()
    for a in range(2):
        gather_done(a)
        scatter_done(a)
    for copy in list(pairs.values()) + list(fars.values()):
        copy.wait_send()


def layer(tokens, out_grad, wg, wu, wd, gtab, dtab, rows, cols, drows, dcols, gcount, dcount, n, nd):
    ntok, width = tokens.shape
    slots, blk, _ = wg.shape
    share = slots // nd
    ny = nd // 2
    nz = n // 2
    hblocks = HID_DEV // blk
    per = width // blk
    rxb = (cross_first(per, "ffn_out"), cross_first(per, "input_grad"))
    parts = slot_parts(share)
    bunch = share // parts
    swap = ny == 2
    kinds = 1 if swap else 3
    dma = pltpu.SemaphoreType.DMA
    return pl.pallas_call(
        functools.partial(layer_kernel, n, nd, 1.0 / math.sqrt(ntok * nd)),
        out_shape=(
            pltpu.VMEM((ntok, width), BF16),
            pltpu.VMEM((ntok, width), BF16),
            pltpu.VMEM((3, share, blk, blk), F32),
        ),
        in_specs=[pl.BlockSpec(memory_space=pltpu.SMEM)] * 8
        + [pl.BlockSpec(memory_space=pl.ANY)] * 5,
        out_specs=(pl.BlockSpec(memory_space=pltpu.VMEM),) * 3,
        scratch_shapes=[
            pltpu.VMEM((n * per, ntok, blk), BF16),
            pltpu.VMEM((n * per, ntok, blk), BF16),
            pltpu.VMEM((slots + 1, blk, blk), BF16),
            pltpu.VMEM((slots + 1, blk, blk), BF16),
            pltpu.VMEM((slots + 1, blk, blk), BF16),
            pltpu.VMEM((hblocks, ntok, 2 * blk), F32),
            pltpu.VMEM((hblocks, ntok, blk), F32),
            pltpu.VMEM((ntok, hblocks * blk), BF16),
            pltpu.VMEM((ntok, 2 * hblocks * blk), BF16),
            pltpu.VMEM((hblocks, ntok, blk), BF16),
            pltpu.VMEM((hblocks, ntok, 2 * blk), BF16),
            pltpu.VMEM((n * per, ntok, blk), BF16),
            pltpu.VMEM((n * per, ntok, blk), BF16),
            *[pltpu.VMEM((nz + 1, per - xb, ntok, blk), BF16) for xb in rxb],
            *[pltpu.VMEM((nz + 1, 2 * xb, ntok, blk), BF16) for xb in rxb],
            *[pltpu.VMEM((nz, per - xb, ntok, blk), BF16) for xb in rxb],
            *[pltpu.VMEM((xb, ntok, blk), BF16) for xb in rxb],
            pltpu.VMEM((ny, 2, parts, kinds, bunch, blk, blk), BF16),
            pltpu.VMEM((ny, parts, kinds, bunch, blk, blk), BF16),
            pltpu.VMEM((max(ny - 1, 1), parts, kinds, bunch, blk, blk), BF16),
            pltpu.VMEM((2, ntok, width), BF16),
            pltpu.VMEM((n * per if swap else 1, ntok, blk), BF16),
            pltpu.VMEM((hblocks if swap else 1, ntok, 2 * blk), BF16),
            pltpu.VMEM((2, parts, 2, bunch, blk, blk) if swap else (1, 1, 1, 1, blk, blk), BF16),
            pltpu.VMEM((parts, 2, bunch, blk, blk) if swap else (1, 1, 1, blk, blk), BF16),
            dma((2,)),
            dma((3,)),
            dma((2, nz)), dma((2, nz)), dma((2,)), dma((2,)),
            dma((2, 2, nz)), dma((2, nz)), dma((2, 2, nz)), dma((2, nz)),
            dma((2, nz)), dma((2, nz)), dma((2,)), dma((2,)),
            dma((2, nz)), dma((2, nz + 1)), dma((2, nz)), dma((2, nz + 1)),
            dma((ny, parts)), dma((ny, parts)), dma((ny, parts)), dma((ny, parts)),
            dma((3, nz)), dma((3, nz)), dma((2,)), dma((parts,)), dma((parts,)),
        ],
        compiler_params=pltpu.CompilerParams(
            collective_id=0, has_side_effects=True, vmem_limit_bytes=56 << 20
        ),
    )(gtab, dtab, rows, cols, drows, dcols, gcount, dcount, tokens, out_grad, wg, wu, wd)


def slot_table(features, hidden, count, dblocks, hblocks):
    slot = jnp.arange(features.shape[0])
    key = jnp.where(slot < count[0], features * hblocks + hidden, -1)
    hit = key[None, :] == jnp.arange(dblocks * hblocks)[:, None]
    return jnp.sum(jnp.where(hit, slot[None, :] + 1, 0), axis=1).astype(jnp.int32)


def hand_over_kernel(ffn_ref, in_ref, step_ref, ffn_out, input_grad, gate_step, up_step, down_step, sems):
    copies = [
        pltpu.make_async_copy(src, dst, sems.at[k])
        for k, (src, dst) in enumerate(
            (
                (step_ref.at[0], gate_step.at[0]),
                (step_ref.at[1], up_step.at[0]),
                (step_ref.at[2], down_step.at[0]),
                (ffn_ref, ffn_out),
                (in_ref, input_grad),
            )
        )
    ]
    for copy in copies:
        copy.start()
    for copy in copies:
        copy.wait()


def hand_over(ffn, inp, steps):
    one = jax.ShapeDtypeStruct((1,) + steps.shape[1:], F32)
    return pl.pallas_call(
        hand_over_kernel,
        out_shape=(
            jax.ShapeDtypeStruct(ffn.shape, BF16),
            jax.ShapeDtypeStruct(inp.shape, BF16),
            one, one, one,
        ),
        in_specs=[pl.BlockSpec(memory_space=pl.ANY)] * 3,
        out_specs=(pl.BlockSpec(memory_space=pl.ANY),) * 5,
        scratch_shapes=[pltpu.SemaphoreType.DMA((5,))],
        compiler_params=pltpu.CompilerParams(vmem_limit_bytes=1 << 20),
    )(ffn, inp, steps)


def local(
    tokens, out_grad, w_gate, w_up, w_down, gu_rows, gu_cols, gu_count, dn_rows, dn_cols, dn_count
):
    n = lax.axis_size("mp")
    nd = lax.axis_size("dp")
    wg, wu, wd = w_gate[0], w_up[0], w_down[0]
    blk = wg.shape[-1]
    dblocks = tokens.shape[1] * n // blk
    hblocks = HID_DEV // blk
    gtab = slot_table(gu_rows[0], gu_cols[0], gu_count, dblocks, hblocks)
    dtab = slot_table(dn_cols[0], dn_rows[0], dn_count, dblocks, hblocks)
    ffn, inp, steps = layer(
        tokens, out_grad, wg, wu, wd, gtab, dtab,
        gu_rows[0], gu_cols[0], dn_rows[0], dn_cols[0], gu_count, dn_count, n, nd,
    )
    return hand_over(ffn, inp, steps)


def solution(mesh):
    in_specs = (
        P("dp", "mp"),
        P("dp", "mp"),
        P("mp", None, None, None),
        P("mp", None, None, None),
        P("mp", None, None, None),
        P("mp", None),
        P("mp", None),
        P("mp"),
        P("mp", None),
        P("mp", None),
        P("mp"),
    )
    out_specs = (
        P("dp", "mp"),
        P("dp", "mp"),
        P("mp", "dp", None, None),
        P("mp", "dp", None, None),
        P("mp", "dp", None, None),
    )
    return jax.shard_map(local, mesh=mesh, in_specs=in_specs, out_specs=out_specs, check_vma=False)
```
